32 devices in a mesh: groups: 2 (over y), patch: 4 (over z), fsdp: 2 (over x), sub: 2 (over core).
Axes of the slice: x: 2, y: 2, z: 4, core: 2. Of those that a mesh axis runs over, the one named last changes fastest.
Arguments:
- noisy_field: float32 [128, 512], P(('groups', 'patch'), 'sub'), parts along dimension 0, may hold values from -6 to 6
- noise_draw: float32 [128, 512], P(('groups', 'patch'), 'sub'), parts along dimension 0, may hold values from -6 to 6
- cond_features: bfloat16 [128, 512, 128], P(('groups', 'patch'), 'sub'), parts along dimension 0, may hold values from -6 to 6
- sigma_now: float32 [1], replicated, may hold values from 0.5 to 2
- sigma_next: float32 [1], replicated, may hold values from 0.1 to 0.4
- field_proj: float32 [128], replicated, may hold values from -6 to 6
- fine_kernels: bfloat16 [2, 9, 128, 128], replicated, may hold values from -0.1875 to 0.1875
- coarse_kernel: bfloat16 [9, 256, 256], replicated, may hold values from -0.125 to 0.125
- down_proj: bfloat16 [128, 256], replicated, may hold values from -0.5 to 0.5
- up_proj: bfloat16 [256, 128], replicated, may hold values from -0.375 to 0.375
- out_proj: bfloat16 [128], replicated, may hold values from -0.5 to 0.5
Outputs:
- next_field: float32 [128, 512], P(('groups', 'patch'), 'sub'), parts along dimension 0
The draws below stay inside these ranges and needn't reach their ends.
There are 2 independent parts, one for each index of `groups`. The reference program is written for one: setup_inputs(seed, part) draws one part's arguments, and reference() takes and returns one part's arrays. A program takes and returns all parts, laid end to end along the dimension named above; an argument that names none is the same for every part. Nothing has to cross between parts.
All inputs are finite; a program needn't handle non-finite values.
Results may differ from the reference program's by a relative error of at most 0.008.
Values may be sent and summed in bfloat16 or wider, within the bound.
No kernel may reach another device: no remote copies, remote signals or barrier semaphores. Data moves between devices by JAX's collectives and lax.ppermute only.
A program may use at most 64 MiB of HBM per device.

```python
import math
import jax
import jax.numpy as jnp
from jax import lax

C1 = 128
C2 = 256
NR = 64
NC = 512


def shard_levels(rng, extent, pieces, smallest, high):
    loudness = 1.0
    for axis_at, blocks in pieces:
        heights = jax.random.uniform(jax.random.fold_in(jax.random.fold_in(rng, 6), axis_at), (blocks,), jnp.float32, smallest / len(pieces), high / len(pieces))
        loudness = loudness * jnp.repeat(jnp.exp(heights), extent[axis_at] // blocks).reshape((-1,) + (1,) * (len(extent) - 1 - axis_at))
    return loudness


def noise(own_key, shape, width, reach, split=(), kind=jnp.bfloat16):
    entries = width * jax.random.normal(own_key, shape, jnp.float32)
    if split:
        entries = entries * shard_levels(own_key, shape, split, -0.22, 0.18)
    return jnp.clip(entries, -reach, reach).astype(kind)


def setup_inputs(seed: int = 0, part: int = 0) -> dict:
    key_of = jax.random.split(jax.random.key(seed), 12)
    part_splits = jax.random.split(jax.random.fold_in(key_of[11], part), 12)
    return {
        "noisy_field": noise(part_splits[0], (NR, NC), 1.0, 6.0, ((0, 4), (1, 2)), jnp.float32),
        "noise_draw": noise(part_splits[1], (NR, NC), 1.0, 6.0, ((0, 4), (1, 2)), jnp.float32),
        "cond_features": noise(part_splits[2], (NR, NC, C1), 1.0, 6.0, ((0, 4), (1, 2))),
        "sigma_now": jnp.clip(jnp.exp(jax.random.uniform(key_of[3], (1,), jnp.float32, math.log(0.5), math.log(2.0))), 0.5, 2.0),
        "sigma_next": jnp.clip(jnp.exp(jax.random.uniform(key_of[4], (1,), jnp.float32, math.log(0.1), math.log(0.4))), 0.1, 0.4),
        "field_proj": noise(key_of[5], (C1,), 1 ** -0.5, 6.0, (), jnp.float32),
        "fine_kernels": noise(key_of[6], (2, 9, C1, C1), (9 * C1) ** -0.5, 0.1875),
        "coarse_kernel": noise(key_of[7], (9, C2, C2), (9 * C2) ** -0.5, 0.125),
        "down_proj": noise(key_of[8], (C1, C2), C1 ** -0.5, 0.5),
        "up_proj": noise(key_of[9], (C2, C1), C2 ** -0.5, 0.375),
        "out_proj": noise(key_of[10], (C1,), C1 ** -0.5, 0.5),
    }


def conv_full(values, kernel):
    height = values.shape[0]
    breadth = values.shape[1]
    channels = values.shape[2]
    padded = jnp.pad(values, ((1, 1), (1, 1), (0, 0)))
    summed = jnp.zeros((height * breadth, kernel.shape[2]), jnp.float32)
    for kernel_tap in range(9):
        row_off = kernel_tap // 3
        col_off = kernel_tap % 3
        window = padded[row_off:row_off + height, col_off:col_off + breadth, :].reshape(height * breadth, channels)
        summed = summed + jnp.dot(window, kernel[kernel_tap], preferred_element_type=jnp.float32)
    return summed.reshape(height, breadth, kernel.shape[2])

def reference(noisy_field, noise_draw, cond_features, sigma_now, sigma_next, field_proj, fine_kernels, coarse_kernel, down_proj, up_proj, out_proj):
    height = noisy_field.shape[0]
    breadth = noisy_field.shape[1]
    level_now = sigma_now[0]
    level_next = sigma_next[0]
    scale_in = 1.0 / jnp.sqrt(level_now * level_now + 1.0)
    scale_skip = 1.0 / (level_now * level_now + 1.0)
    scale_out = level_now * scale_in
    hidden0 = (cond_features.astype(jnp.float32) + (scale_in * noisy_field)[:, :, None] * field_proj).astype(jnp.bfloat16)
    hidden1 = (hidden0.astype(jnp.float32) + jax.nn.silu(conv_full(hidden0, fine_kernels[0]))).astype(jnp.bfloat16)
    pooled = hidden1.astype(jnp.float32).reshape(height // 2, 2, breadth // 2, 2, C1).mean(axis=(1, 3)).astype(jnp.bfloat16)
    coarse_in = jnp.dot(pooled.reshape(-1, C1), down_proj, preferred_element_type=jnp.float32).astype(jnp.bfloat16).reshape(height // 2, breadth // 2, C2)
    coarse_out = (coarse_in.astype(jnp.float32) + jax.nn.silu(conv_full(coarse_in, coarse_kernel))).astype(jnp.bfloat16)
    lifted = jnp.dot(coarse_out.reshape(-1, C2), up_proj, preferred_element_type=jnp.float32).reshape(height // 2, breadth // 2, C1)
    lifted = jnp.repeat(jnp.repeat(lifted, 2, axis=0), 2, axis=1)
    hidden2 = (hidden1.astype(jnp.float32) + lifted).astype(jnp.bfloat16)
    hidden3 = (hidden2.astype(jnp.float32) + jax.nn.silu(conv_full(hidden2, fine_kernels[1]))).astype(jnp.bfloat16)
    network = lax.optimization_barrier(jnp.sum(hidden3.astype(jnp.float32) * out_proj.astype(jnp.float32), axis=2))
    denoised = scale_skip * noisy_field + scale_out * network
    ratio = level_next / level_now
    spread = jnp.sqrt(level_now * level_now - level_next * level_next)
    return denoised + ratio * (noisy_field - denoised) + spread * noise_draw
```

```python
import functools

import jax
import jax.numpy as jnp
from jax import lax
from jax.experimental import pallas as pl
from jax.experimental.pallas import tpu as pltpu
from jax.sharding import PartitionSpec as P

F32 = jnp.float32
BF16 = jnp.bfloat16
HALO = 5
EDGE = 16
PER = EDGE // 2


def silu(v):
    half = 0.5 * v
    return half + half * jnp.tanh(half)


def column_mask(ring, own, index, count):
    at = lax.broadcasted_iota(jnp.int32, (ring, 128), 0)
    right = jnp.where(index < count - 1, 1, 0)
    left = jnp.where(index > 0, 1, 0)
    inside = jnp.where(at < own, 1, jnp.where(at < own + PER, right, left))
    return inside.astype(F32)


def embed_kernel(now_ref, cond_ref, noisy_ref, proj_ref, left_ref, right_ref, out_ref, wide, edge, *, sub, count):
    rows, cols, _ = cond_ref.shape
    index = lax.axis_index(sub)
    level = jnp.full((1, 128), now_ref[0], F32)
    scale_in = 1.0 / jnp.sqrt(level * level + 1.0)
    noisy = noisy_ref[...] * scale_in[:, :1]
    turned = jnp.transpose(noisy)
    proj = proj_ref[...]
    keep_left = jnp.where(index > 0, 1.0, 0.0).astype(F32)
    keep_right = jnp.where(index < count - 1, 1.0, 0.0).astype(F32)
    for r in range(rows):
        wide[r % 2] = cond_ref[r].astype(F32) + turned[:, r : r + 1] * proj
        edge[r % 2, :EDGE] = left_ref[r].astype(F32) * keep_left
        edge[r % 2, EDGE:] = right_ref[r].astype(F32) * keep_right
        for q in range(2):
            main = wide[r % 2, pl.ds(q, cols // 2, stride=2), :]
            lt = edge[r % 2, pl.ds(q, PER, stride=2), :]
            rt = edge[r % 2, pl.ds(EDGE + q, PER, stride=2), :]
            out_ref[r, q] = jnp.concatenate([main, rt, lt], axis=0).astype(BF16)


def step_kernel(
    now_ref, next_ref, own_ref, top_ref, bot_ref, fine_ref, coarse_ref, down_ref, up_ref, outp_ref,
    noisy_ref, noise_ref, out_ref,
    x_ref, w_ref, h1_ref, pool_ref, ci_ref, co_ref, h2_ref, h3_ref, flat_ref,
    *, patch, patches, sub, subs,
):
    rows, _, ring, c1 = own_ref.shape
    own = out_ref.shape[1] // 2
    c2 = down_ref.shape[1]
    p = lax.axis_index(patch)
    s = lax.axis_index(sub)
    inside = column_mask(ring, own, s, subs)
    above = jnp.where(p > 0, 1.0, 0.0).astype(F32)
    below = jnp.where(p < patches - 1, 1.0, 0.0).astype(F32)

    def row_mask(r, extent):
        if r < 0:
            return inside * above
        if r >= extent:
            return inside * below
        return inside

    for layer in range(2):
        for b in range(3):
            for d in range(4):
                at = (b * 4 + d) * c1
                for o in range(2):
                    a = d - o
                    block = fine_ref[layer, a * 3 + b] if 0 <= a <= 2 else jnp.zeros((c1, c1), BF16)
                    w_ref[layer, at : at + c1, o * c1 : (o + 1) * c1] = block

    def put_planes(ref, at, even, odd):
        ref[at, 0] = even.astype(BF16)
        ref[at, 1] = odd.astype(BF16)
        ref[at, 2] = pltpu.roll(odd, 1, 0).astype(BF16)
        ref[at, 3] = pltpu.roll(even, ring - 1, 0).astype(BF16)

    for r in range(-HALO, rows + HALO):
        src, at = (top_ref, r + HALO) if r < 0 else (own_ref, r) if r < rows else (bot_ref, r - rows)
        put_planes(x_ref, r + HALO, src[at, 0].astype(F32), src[at, 1].astype(F32))

    def conv_pair(ref, at, layer):
        parts = []
        for planes in ((2, 0, 1), (0, 1, 3)):
            parts.append(jnp.concatenate([ref[at + d, k] for k in planes for d in range(4)], axis=1))
        lhs = jnp.concatenate(parts, axis=0)
        return jnp.dot(lhs, w_ref[layer], preferred_element_type=F32)

    half = rows // 2
    for i in range(-2, half + 2):
        acc = conv_pair(x_ref, 2 * i - 1 + HALO, 0)
        total = None
        for o in range(2):
            for q in range(2):
                v = acc[q * ring : (q + 1) * ring, o * c1 : (o + 1) * c1]
                h = (x_ref[2 * i + o + HALO, q].astype(F32) + silu(v)).astype(BF16)
                if -1 <= 2 * i + o <= rows:
                    h1_ref[2 * i + o + 1, q] = h
                total = h.astype(F32) if total is None else total + h.astype(F32)
        pool_ref[(i + 2) * ring : (i + 3) * ring] = (total * 0.25).astype(BF16)

    for i in range(-2, half + 2):
        ci = jnp.dot(pool_ref[(i + 2) * ring : (i + 3) * ring], down_ref[...], preferred_element_type=F32)
        mask = row_mask(i, half)
        ci = ci * jnp.concatenate([mask] * (c2 // 128), axis=1)
        ci_ref[i + 2, 0] = pltpu.roll(ci, 1, 0).astype(BF16)
        ci_ref[i + 2, 1] = ci.astype(BF16)
        ci_ref[i + 2, 2] = pltpu.roll(ci, ring - 1, 0).astype(BF16)
    for i in range(-1, half + 1):
        lhs = jnp.concatenate([ci_ref[i + 1 + a, b] for a in range(3) for b in range(3)], axis=1)
        v = jnp.dot(lhs, coarse_ref[...], preferred_element_type=F32)
        co = (ci_ref[i + 2, 1].astype(F32) + silu(v)).astype(BF16)
        co_ref[(i + 1) * ring : (i + 2) * ring] = co

    for i in range(-1, half + 1):
        lifted = jnp.dot(co_ref[(i + 1) * ring : (i + 2) * ring], up_ref[...], preferred_element_type=F32)
        for o in range(2):
            r = 2 * i + o
            if -1 <= r <= rows:
                mask = row_mask(r, rows)
                put_planes(
                    h2_ref, r + 1,
                    (h1_ref[r + 1, 0].astype(F32) + lifted) * mask,
                    (h1_ref[r + 1, 1].astype(F32) + lifted) * mask,
                )

    for i in range(half):
        acc = conv_pair(h2_ref, 2 * i, 1)
        for o in range(2):
            for q in range(2):
                v = acc[q * ring : (q + 1) * ring, o * c1 : (o + 1) * c1]
                h = h2_ref[2 * i + o + 1, q].astype(F32) + silu(v)
                h3_ref[q, 2 * i + o] = h[:own].astype(BF16)

    spread = jnp.transpose(jnp.broadcast_to(outp_ref[...].astype(F32), (128, c1)))
    lane = lax.broadcasted_iota(jnp.int32, (c1, 128), 1)
    pick = jnp.concatenate([jnp.where(lane == r, spread, 0.0).astype(BF16) for r in range(rows)], axis=0)
    for q in range(2):
        lhs = jnp.concatenate([h3_ref[q, r] for r in range(rows)], axis=1)
        flat_ref[pl.ds(q, own, stride=2), :] = jnp.dot(lhs, pick, preferred_element_type=F32)
    network = jnp.transpose(flat_ref[...])[:rows]

    level = jnp.full((1, 128), now_ref[0], F32)
    after = jnp.full((1, 128), next_ref[0], F32)
    scale_in = 1.0 / jnp.sqrt(level * level + 1.0)
    scale_skip = (1.0 / (level * level + 1.0))[:, :1]
    scale_out = (level * scale_in)[:, :1]
    ratio = (after / level)[:, :1]
    spread_by = jnp.sqrt(level * level - after * after)[:, :1]
    noisy = noisy_ref[...]
    denoised = scale_skip * noisy + scale_out * network
    out_ref[...] = denoised + ratio * (noisy - denoised) + spread_by * noise_ref[...]


def per_device(
    sizes,
    noisy_field, noise_draw, cond_features, sigma_now, sigma_next, field_proj,
    fine_kernels, coarse_kernel, down_proj, up_proj, out_proj,
):
    rows, cols, c1 = cond_features.shape
    c2 = down_proj.shape[1]
    patches, subs = sizes["patch"], sizes["sub"]
    own = cols // 2
    ring = own + EDGE
    half = rows // 2
    smem = pl.BlockSpec(memory_space=pltpu.SMEM)
    vmem = pl.BlockSpec(memory_space=pltpu.VMEM)
    level = sigma_now[0]
    scale_in = 1.0 / jnp.sqrt(level * level + 1.0)

    def edge_at(start):
        cond = lax.dynamic_slice_in_dim(cond_features, start, EDGE, 1)
        noisy = lax.dynamic_slice_in_dim(noisy_field, start, EDGE, 1)
        return (cond.astype(F32) + (scale_in * noisy)[:, :, None] * field_proj).astype(BF16)

    if subs == 2:
        start = jnp.where(lax.axis_index("sub") == 0, cols - EDGE, 0)
        left = right = lax.ppermute(edge_at(start), "sub", [(0, 1), (1, 0)])
    else:
        left = lax.ppermute(edge_at(cols - EDGE), "sub", [(i, i + 1) for i in range(subs - 1)])
        right = lax.ppermute(edge_at(0), "sub", [(i + 1, i) for i in range(subs - 1)])

    mine = pl.pallas_call(
        functools.partial(embed_kernel, sub="sub", count=subs),
        out_shape=jax.ShapeDtypeStruct((rows, 2, ring, c1), BF16),
        in_specs=[smem] + [vmem] * 5,
        out_specs=vmem,
        scratch_shapes=[pltpu.VMEM((2, cols, c1), F32), pltpu.VMEM((2, 2 * EDGE, c1), F32)],
        name="embed",
    )(sigma_now, cond_features, noisy_field, field_proj[None], left, right)

    top = lax.ppermute(mine[rows - HALO :], "patch", [(i, i + 1) for i in range(patches - 1)])
    bot = lax.ppermute(mine[:HALO], "patch", [(i + 1, i) for i in range(patches - 1)])

    return pl.pallas_call(
        functools.partial(step_kernel, patch="patch", patches=patches, sub="sub", subs=subs),
        out_shape=jax.ShapeDtypeStruct((rows, cols), F32),
        in_specs=[smem, smem] + [vmem] * 10,
        out_specs=vmem,
        scratch_shapes=[
            pltpu.VMEM((rows + 2 * HALO, 4, ring, c1), BF16),
            pltpu.VMEM((2, 12 * c1, 2 * c1), BF16),
            pltpu.VMEM((rows + 2, 2, ring, c1), BF16),
            pltpu.VMEM(((half + 4) * ring, c1), BF16),
            pltpu.VMEM((half + 4, 3, ring, c2), BF16),
            pltpu.VMEM(((half + 2) * ring, c2), BF16),
            pltpu.VMEM((rows + 2, 4, ring, c1), BF16),
            pltpu.VMEM((2, rows, own, c1), BF16),
            pltpu.VMEM((cols, 128), F32),
        ],
        name="step",
    )(
        sigma_now, sigma_next, mine, top, bot, fine_kernels, coarse_kernel.reshape(9 * c2, c2),
        down_proj, up_proj, out_proj[None], noisy_field, noise_draw,
    )


def solution(mesh):
    return jax.shard_map(
        functools.partial(per_device, dict(mesh.shape)),
        mesh=mesh,
        in_specs=(
            P(("groups", "patch"), "sub"),
            P(("groups", "patch"), "sub"),
            P(("groups", "patch"), "sub", None),
            P(),
            P(),
            P(),
            P(),
            P(),
            P(),
            P(),
            P(),
        ),
        out_specs=P(("groups", "patch"), "sub"),
        check_vma=False,
    )
```

```python
import functools

import jax
import jax.numpy as jnp
from jax import lax
from jax.experimental import pallas as pl
from jax.experimental.pallas import tpu as pltpu
from jax.sharding import PartitionSpec as P

F32 = jnp.float32
BF16 = jnp.bfloat16
HALO = 5
EDGE = 16
PER = EDGE // 2


def silu(v):
    half = 0.5 * v
    return half + half * jnp.tanh(half)


def column_mask(ring, own, index, count):
    at = lax.broadcasted_iota(jnp.int32, (ring, 128), 0)
    right = jnp.where(index < count - 1, 1, 0)
    left = jnp.where(index > 0, 1, 0)
    inside = jnp.where(at < own, 1, jnp.where(at < own + PER, right, left))
    return inside.astype(F32)


def embed_kernel(now_ref, cond_ref, noisy_ref, proj_ref, left_ref, right_ref, out_ref, up_ref, dn_ref, wide, edge, *, sub, count):
    rows, cols, _ = cond_ref.shape
    index = lax.axis_index(sub)
    level = jnp.full((1, 128), now_ref[0], F32)
    scale_in = 1.0 / jnp.sqrt(level * level + 1.0)
    noisy = noisy_ref[...] * scale_in[:, :1]
    turned = jnp.transpose(noisy)
    proj = proj_ref[...]
    keep_left = jnp.where(index > 0, 1.0, 0.0).astype(F32)
    keep_right = jnp.where(index < count - 1, 1.0, 0.0).astype(F32)
    for r in range(rows):
        wide[r % 2] = cond_ref[r].astype(F32) + turned[:, r : r + 1] * proj
        edge[r % 2, :EDGE] = left_ref[r].astype(F32) * keep_left
        edge[r % 2, EDGE:] = right_ref[r].astype(F32) * keep_right
        for q in range(2):
            main = wide[r % 2, pl.ds(q, cols // 2, stride=2), :]
            lt = edge[r % 2, pl.ds(q, PER, stride=2), :]
            rt = edge[r % 2, pl.ds(EDGE + q, PER, stride=2), :]
            full = jnp.concatenate([main, rt, lt], axis=0).astype(BF16)
            out_ref[r, q] = full
            if r < HALO:
                dn_ref[r, q] = full
            if r >= rows - HALO:
                up_ref[r - rows + HALO, q] = full


def step_kernel(
    now_ref, next_ref, own_ref, top_ref, bot_ref, fine_ref, coarse_ref, down_ref, up_ref, outp_ref,
    noisy_ref, noise_ref, out_ref,
    x_ref, w_ref, h1_ref, pool_ref, ci_ref, co_ref, h2_ref, h3_ref, flat_ref,
    *, patch, patches, sub, subs,
):
    rows, _, ring, c1 = own_ref.shape
    own = out_ref.shape[1] // 2
    c2 = down_ref.shape[1]
    p = lax.axis_index(patch)
    s = lax.axis_index(sub)
    inside = column_mask(ring, own, s, subs)
    above = jnp.where(p > 0, 1.0, 0.0).astype(F32)
    below = jnp.where(p < patches - 1, 1.0, 0.0).astype(F32)

    def row_mask(r, extent):
        if r < 0:
            return inside * above
        if r >= extent:
            return inside * below
        return inside

    for layer in range(2):
        for b in range(3):
            for d in range(4):
                at = (b * 4 + d) * c1
                for o in range(2):
                    a = d - o
                    block = fine_ref[layer, a * 3 + b] if 0 <= a <= 2 else jnp.zeros((c1, c1), BF16)
                    w_ref[layer, at : at + c1, o * c1 : (o + 1) * c1] = block

    def put_planes(ref, at, even, odd):
        ref[at, 0] = even.astype(BF16)
        ref[at, 1] = odd.astype(BF16)
        ref[at, 2] = pltpu.roll(odd, 1, 0).astype(BF16)
        ref[at, 3] = pltpu.roll(even, ring - 1, 0).astype(BF16)

    for r in range(-HALO, rows + HALO):
        src, at = (top_ref, r + HALO) if r < 0 else (own_ref, r) if r < rows else (bot_ref, r - rows)
        put_planes(x_ref, r + HALO, src[at, 0].astype(F32), src[at, 1].astype(F32))

    def conv_pair(ref, at, layer):
        parts = []
        for planes in ((2, 0, 1), (0, 1, 3)):
            parts.append(jnp.concatenate([ref[at + d, k] for k in planes for d in range(4)], axis=1))
        lhs = jnp.concatenate(parts, axis=0)
        return jnp.dot(lhs, w_ref[layer], preferred_element_type=F32)

    half = rows // 2
    for i in range(-2, half + 2):
        acc = conv_pair(x_ref, 2 * i - 1 + HALO, 0)
        total = None
        for o in range(2):
            for q in range(2):
                v = acc[q * ring : (q + 1) * ring, o * c1 : (o + 1) * c1]
                h = (x_ref[2 * i + o + HALO, q].astype(F32) + silu(v)).astype(BF16)
                if -1 <= 2 * i + o <= rows:
                    h1_ref[2 * i + o + 1, q] = h
                total = h.astype(F32) if total is None else total + h.astype(F32)
        pool_ref[(i + 2) * ring : (i + 3) * ring] = (total * 0.25).astype(BF16)

    for i in range(-2, half + 2):
        ci = jnp.dot(pool_ref[(i + 2) * ring : (i + 3) * ring], down_ref[...], preferred_element_type=F32)
        mask = row_mask(i, half)
        ci = ci * jnp.concatenate([mask] * (c2 // 128), axis=1)
        ci_ref[i + 2, 0] = pltpu.roll(ci, 1, 0).astype(BF16)
        ci_ref[i + 2, 1] = ci.astype(BF16)
        ci_ref[i + 2, 2] = pltpu.roll(ci, ring - 1, 0).astype(BF16)
    for i in range(-1, half + 1):
        lhs = jnp.concatenate([ci_ref[i + 1 + a, b] for a in range(3) for b in range(3)], axis=1)
        v = jnp.dot(lhs, coarse_ref[...], preferred_element_type=F32)
        co = (ci_ref[i + 2, 1].astype(F32) + silu(v)).astype(BF16)
        co_ref[(i + 1) * ring : (i + 2) * ring] = co

    for i in range(-1, half + 1):
        lifted = jnp.dot(co_ref[(i + 1) * ring : (i + 2) * ring], up_ref[...], preferred_element_type=F32)
        for o in range(2):
            r = 2 * i + o
            if -1 <= r <= rows:
                mask = row_mask(r, rows)
                put_planes(
                    h2_ref, r + 1,
                    (h1_ref[r + 1, 0].astype(F32) + lifted) * mask,
                    (h1_ref[r + 1, 1].astype(F32) + lifted) * mask,
                )

    for i in range(half):
        acc = conv_pair(h2_ref, 2 * i, 1)
        for o in range(2):
            for q in range(2):
                v = acc[q * ring : (q + 1) * ring, o * c1 : (o + 1) * c1]
                h = h2_ref[2 * i + o + 1, q].astype(F32) + silu(v)
                h3_ref[q, 2 * i + o] = h[:own].astype(BF16)

    spread = jnp.transpose(jnp.broadcast_to(outp_ref[...].astype(F32), (128, c1)))
    lane = lax.broadcasted_iota(jnp.int32, (c1, 128), 1)
    pick = jnp.concatenate([jnp.where(lane == r, spread, 0.0).astype(BF16) for r in range(rows)], axis=0)
    for q in range(2):
        lhs = jnp.concatenate([h3_ref[q, r] for r in range(rows)], axis=1)
        flat_ref[pl.ds(q, own, stride=2), :] = jnp.dot(lhs, pick, preferred_element_type=F32)
    network = jnp.transpose(flat_ref[...])[:rows]

    level = jnp.full((1, 128), now_ref[0], F32)
    after = jnp.full((1, 128), next_ref[0], F32)
    scale_in = 1.0 / jnp.sqrt(level * level + 1.0)
    scale_skip = (1.0 / (level * level + 1.0))[:, :1]
    scale_out = (level * scale_in)[:, :1]
    ratio = (after / level)[:, :1]
    spread_by = jnp.sqrt(level * level - after * after)[:, :1]
    noisy = noisy_ref[...]
    denoised = scale_skip * noisy + scale_out * network
    out_ref[...] = denoised + ratio * (noisy - denoised) + spread_by * noise_ref[...]


def near(*arrays):
    return [pltpu.with_memory_space_constraint(a, pltpu.VMEM) for a in arrays]


def per_device(
    sizes,
    noisy_field, noise_draw, cond_features, sigma_now, sigma_next, field_proj,
    fine_kernels, coarse_kernel, down_proj, up_proj, out_proj,
):
    rows, cols, c1 = cond_features.shape
    c2 = down_proj.shape[1]
    patches, subs = sizes["patch"], sizes["sub"]
    own = cols // 2
    ring = own + EDGE
    half = rows // 2
    smem = pl.BlockSpec(memory_space=pltpu.SMEM)
    vmem = pl.BlockSpec(memory_space=pltpu.VMEM)
    level = sigma_now[0]
    scale_in = 1.0 / jnp.sqrt(level * level + 1.0)

    def edge_at(start):
        cond = lax.dynamic_slice_in_dim(cond_features, start, EDGE, 1)
        noisy = lax.dynamic_slice_in_dim(noisy_field, start, EDGE, 1)
        return (cond.astype(F32) + (scale_in * noisy)[:, :, None] * field_proj).astype(BF16)

    if subs == 2:
        start = jnp.where(lax.axis_index("sub") == 0, cols - EDGE, 0)
        left = right = lax.ppermute(edge_at(start), "sub", [(0, 1), (1, 0)])
    else:
        left = lax.ppermute(edge_at(cols - EDGE), "sub", [(i, i + 1) for i in range(subs - 1)])
        right = lax.ppermute(edge_at(0), "sub", [(i + 1, i) for i in range(subs - 1)])

    mine, upward, downward = pl.pallas_call(
        functools.partial(embed_kernel, sub="sub", count=subs),
        out_shape=[pltpu.VMEM((n, 2, ring, c1), BF16) for n in (rows, HALO, HALO)],
        in_specs=[smem] + [vmem] * 5,
        out_specs=[vmem] * 3,
        scratch_shapes=[pltpu.VMEM((2, cols, c1), F32), pltpu.VMEM((2, 2 * EDGE, c1), F32)],
        compiler_params=pltpu.CompilerParams(vmem_limit_bytes=24 << 20),
        name="embed",
    )(sigma_now, cond_features, noisy_field, field_proj[None], *near(left, right))

    top = lax.ppermute(upward, "patch", [(i, i + 1) for i in range(patches - 1)])
    bot = lax.ppermute(downward, "patch", [(i + 1, i) for i in range(patches - 1)])

    return pl.pallas_call(
        functools.partial(step_kernel, patch="patch", patches=patches, sub="sub", subs=subs),
        out_shape=jax.ShapeDtypeStruct((rows, cols), F32),
        in_specs=[smem, smem] + [vmem] * 10,
        out_specs=vmem,
        scratch_shapes=[
            pltpu.VMEM((rows + 2 * HALO, 4, ring, c1), BF16),
            pltpu.VMEM((2, 12 * c1, 2 * c1), BF16),
            pltpu.VMEM((rows + 2, 2, ring, c1), BF16),
            pltpu.VMEM(((half + 4) * ring, c1), BF16),
            pltpu.VMEM((half + 4, 3, ring, c2), BF16),
            pltpu.VMEM(((half + 2) * ring, c2), BF16),
            pltpu.VMEM((rows + 2, 4, ring, c1), BF16),
            pltpu.VMEM((2, rows, own, c1), BF16),
            pltpu.VMEM((cols, 128), F32),
        ],
        compiler_params=pltpu.CompilerParams(vmem_limit_bytes=32 << 20),
        name="step",
    )(
        sigma_now, sigma_next,
        *near(mine, top, bot, fine_kernels, coarse_kernel.reshape(9 * c2, c2), down_proj, up_proj),
        out_proj[None], noisy_field, noise_draw,
    )


def solution(mesh):
    return jax.shard_map(
        functools.partial(per_device, dict(mesh.shape)),
        mesh=mesh,
        in_specs=(
            P(("groups", "patch"), "sub"),
            P(("groups", "patch"), "sub"),
            P(("groups", "patch"), "sub", None),
            P(),
            P(),
            P(),
            P(),
            P(),
            P(),
            P(),
            P(),
        ),
        out_specs=P(("groups", "patch"), "sub"),
        check_vma=False,
    )
```

```python
import functools

import jax
import jax.numpy as jnp
from jax import lax
from jax.experimental import pallas as pl
from jax.experimental.pallas import tpu as pltpu
from jax.sharding import PartitionSpec as P

F32 = jnp.float32
BF16 = jnp.bfloat16
HALO = 5
EDGE = 16
PER = EDGE // 2
CHUNK = 3


def silu(v):
    half = 0.5 * v
    return half + half * jnp.tanh(half)


def flag(condition):
    return jnp.where(condition, 1.0, 0.0).astype(F32)


class Place:
    def __init__(self, sizes, pieces):
        self.piece = lax.rem(lax.axis_index("fsdp"), pieces)
        self.sub = lax.axis_index("sub")
        self.patch = lax.axis_index("patch")
        self.first = self.piece == 0
        self.last = self.piece == pieces - 1
        self.has_left = jnp.logical_or(self.piece > 0, self.sub > 0)
        self.has_right = jnp.logical_or(self.piece < pieces - 1, self.sub < sizes["sub"] - 1)
        self.above = flag(self.patch > 0)
        self.below = flag(self.patch < sizes["patch"] - 1)

    def column_mask(self, ring, own):
        at = lax.broadcasted_iota(jnp.int32, (ring, 128), 0)
        return jnp.where(at < own, 1.0, jnp.where(at < own + PER, flag(self.has_right), flag(self.has_left)))


def embed_kernel(
    now_ref, cond_ref, noisy_ref, proj_ref, mine_ref, tile_ref, send_ref,
    main, inner, give, field, embedding, turned, wide, edge, sems, *, sizes, pieces,
):
    rows, window, _ = main.shape
    cols = noisy_ref.shape[1]
    place = Place(sizes, pieces)
    start = pl.multiple_of(place.piece * window, EDGE)
    near_by = pl.multiple_of(jnp.where(place.first, window, start - EDGE), EDGE)
    given = pl.multiple_of(jnp.where(place.sub == 0, cols - EDGE, 0), EDGE)
    small = [
        pltpu.make_async_copy(noisy_ref, field, sems.at[3]),
        pltpu.make_async_copy(proj_ref, embedding, sems.at[4]),
    ]
    copies = [pltpu.make_async_copy(cond_ref.at[:, pl.ds(given, EDGE)], give, sems.at[0])]
    if pieces > 1:
        copies.append(pltpu.make_async_copy(cond_ref.at[:, pl.ds(near_by, EDGE)], inner, sems.at[1]))
    copies.append(pltpu.make_async_copy(cond_ref.at[:, pl.ds(start, window)], main, sems.at[2]))
    for copy in small + copies:
        copy.start()
    level = jnp.full((1, 128), now_ref[0], F32)
    scale_in = 1.0 / jnp.sqrt(level * level + 1.0)
    for copy in small:
        copy.wait()
    turned[:, :rows] = jnp.transpose(field[...] * scale_in[:, :1])
    proj = embedding[...]

    def hidden(buf, r, at):
        return buf[r].astype(F32) + turned[pl.ds(at, buf.shape[1]), r : r + 1] * proj

    for copy in copies[:-1]:
        copy.wait()
    for r in range(rows):
        edge[r % 2, :EDGE] = hidden(give, r, given)
        for q in range(2):
            send_ref[r, q] = edge[r % 2, pl.ds(q, PER, stride=2), :].astype(BF16)
        if pieces > 1:
            edge[r % 2, EDGE:] = hidden(inner, r, near_by)
            for q in range(2):
                block = edge[r % 2, pl.ds(EDGE + q, PER, stride=2), :]
                to_right = block * flag(jnp.logical_not(place.last))
                to_left = block * flag(jnp.logical_not(place.first))
                tile_ref[r, q] = jnp.concatenate([to_right, to_left], axis=0).astype(BF16)
        else:
            tile_ref[r] = jnp.zeros_like(tile_ref[r])
    copies[-1].wait()
    for r in range(rows):
        wide[r % 2] = hidden(main, r, start)
        for q in range(2):
            mine_ref[r, q] = wide[r % 2, pl.ds(q, window // 2, stride=2), :].astype(BF16)


def border_kernel(mine_ref, tile_ref, got_ref, full_ref, up_ref, down_ref, *, sizes, pieces):
    rows, _, own, _ = mine_ref.shape
    place = Place(sizes, pieces)
    right = flag(jnp.logical_and(place.last, place.has_right))
    left = flag(jnp.logical_and(place.first, place.has_left))
    for r in range(rows):
        for q in range(2):
            got = got_ref[r, q].astype(F32)
            tile = tile_ref[r, q].astype(F32) + jnp.concatenate([got * right, got * left], axis=0)
            tile = tile.astype(BF16)
            full_ref[r, q] = tile
            for ref, at in ((down_ref, r), (up_ref, r - rows + HALO)):
                if 0 <= at < HALO:
                    ref[at, q, :own] = mine_ref[r, q]
                    ref[at, q, own:] = tile


def put_planes(ref, at, even, odd):
    ring = even.shape[0]
    ref[at, 0] = even.astype(BF16)
    ref[at, 1] = odd.astype(BF16)
    ref[at, 2] = pltpu.roll(odd, 1, 0).astype(BF16)
    ref[at, 3] = pltpu.roll(even, ring - 1, 0).astype(BF16)


def chunks(rows_of):
    return [rows_of[k : k + CHUNK] for k in range(0, len(rows_of), CHUNK)]


def conv_pairs(planes_of, pairs, weight):
    parts = []
    for i in pairs:
        found = [planes_of(2 * i - 1 + d) for d in range(4)]
        for planes in ((2, 0, 1), (0, 1, 3)):
            parts.append(jnp.concatenate([ref[at, k] for k in planes for ref, at in found], axis=1))
    return jnp.dot(jnp.concatenate(parts, axis=0), weight[...], preferred_element_type=F32)


def first_conv(planes_of, h1_of, pool_ref, slot_of, pairs, weight, ring, c1):
    for group in chunks(pairs):
        acc = conv_pairs(planes_of, group, weight)
        for n, i in enumerate(group):
            total = None
            for o in range(2):
                ref, at = planes_of(2 * i + o)
                for q in range(2):
                    v = acc[(2 * n + q) * ring : (2 * n + q + 1) * ring, o * c1 : (o + 1) * c1]
                    h = (ref[at, q].astype(F32) + silu(v)).astype(BF16)
                    kept = h1_of(2 * i + o)
                    if kept is not None:
                        kept[0][kept[1], q] = h
                    total = h.astype(F32) if total is None else total + h.astype(F32)
            pool_ref[slot_of(i) * ring : (slot_of(i) + 1) * ring] = (total * 0.25).astype(BF16)


def coarse_in(pool_ref, down_ref, ci_of, order, mask_of, ring, c2):
    ci_all = jnp.dot(pool_ref[...], down_ref[...], preferred_element_type=F32)
    for n, i in enumerate(order):
        ci = ci_all[n * ring : (n + 1) * ring] * jnp.concatenate([mask_of(i)] * (c2 // 128), axis=1)
        ref, at = ci_of(i)
        ref[at, 0] = pltpu.roll(ci, 1, 0).astype(BF16)
        ref[at, 1] = ci.astype(BF16)
        ref[at, 2] = pltpu.roll(ci, ring - 1, 0).astype(BF16)


def coarse_conv(ci_of, co_ref, order, coarse_ref, ring):
    for k, group in enumerate(chunks(order)):
        parts = []
        for i in group:
            found = [ci_of(i - 1 + a) for a in range(3)]
            parts.append(jnp.concatenate([ref[at, b] for ref, at in found for b in range(3)], axis=1))
        v = jnp.dot(jnp.concatenate(parts, axis=0), coarse_ref[...], preferred_element_type=F32)
        for n, i in enumerate(group):
            ref, at = ci_of(i)
            slot = k * CHUNK + n
            co = ref[at, 1].astype(F32) + silu(v[n * ring : (n + 1) * ring])
            co_ref[slot * ring : (slot + 1) * ring] = co.astype(BF16)


def lift(co_ref, up_ref, order, h1_of, h2_of, mask_of, wanted, ring):
    lifted_all = jnp.dot(co_ref[...], up_ref[...], preferred_element_type=F32)
    for n, i in enumerate(order):
        lifted = lifted_all[n * ring : (n + 1) * ring]
        for r in (2 * i, 2 * i + 1):
            if r in wanted:
                ref, at = h1_of(r)
                mask = mask_of(r)
                into, slot = h2_of(r)
                put_planes(into, slot, (ref[at, 0].astype(F32) + lifted) * mask, (ref[at, 1].astype(F32) + lifted) * mask)


def second_conv(h2_of, h3_of, pairs, weight, ring, own, c1):
    for group in chunks(pairs):
        acc = conv_pairs(h2_of, group, weight)
        for n, i in enumerate(group):
            for o in range(2):
                ref, at = h2_of(2 * i + o)
                into, slot = h3_of(2 * i + o)
                for q in range(2):
                    v = acc[(2 * n + q) * ring : (2 * n + q) * ring + own, o * c1 : (o + 1) * c1]
                    into[q, slot] = (ref[at, q, :own].astype(F32) + silu(v)).astype(BF16)


def inner_kernel(
    mine_ref, tile_ref, fine_ref, coarse_ref, down_ref, up_ref,
    x_ref, w_ref, h1_ref, ci_ref, h2_ref, h3_ref, pool_ref, co_ref, *, sizes, pieces,
):
    rows, _, own, c1 = mine_ref.shape
    ring = own + EDGE
    c2 = down_ref.shape[1]
    half = rows // 2
    mask = Place(sizes, pieces).column_mask(ring, own)
    for layer in range(2):
        for b in range(3):
            for d in range(4):
                at = (b * 4 + d) * c1
                for o in range(2):
                    a = d - o
                    block = fine_ref[layer, a * 3 + b] if 0 <= a <= 2 else jnp.zeros((c1, c1), BF16)
                    w_ref[layer, at : at + c1, o * c1 : (o + 1) * c1] = block
    for r in range(rows):
        even, odd = (jnp.concatenate([mine_ref[r, q].astype(F32), tile_ref[r, q].astype(F32)], axis=0) for q in range(2))
        put_planes(x_ref, r, even, odd)
    x_of = lambda r: (x_ref, r)
    h1_of = lambda r: (h1_ref, r - 2)
    ci_of = lambda i: (ci_ref, i - 1)
    h2_of = lambda r: (h2_ref, r - 4)
    h3_of = lambda r: (h3_ref, r - 6)
    first_conv(x_of, h1_of, pool_ref, lambda i: i - 1, list(range(1, half - 1)), w_ref.at[0], ring, c1)
    coarse_in(pool_ref, down_ref, ci_of, range(1, half - 1), lambda i: mask, ring, c2)
    coarse_conv(ci_of, co_ref, list(range(2, half - 2)), coarse_ref, ring)
    lift(co_ref, up_ref, range(2, half - 2), h1_of, h2_of, lambda r: mask, range(4, rows - 4), ring)
    second_conv(h2_of, h3_of, list(range(3, half - 3)), w_ref.at[1], ring, own, c1)


def outer_kernel(
    now_ref, next_ref, top_ref, bot_ref, xin_ref, w_ref, h1in_ref, ciin_ref, h2in_ref, h3in_ref,
    coarse_ref, down_ref, up_ref, outp_ref, noisy_ref, noise_ref, out_ref,
    x_ref, pool_ref, h1_ref, ci_ref, co_ref, h2_ref, h3_ref, flat_ref, *, sizes, pieces,
):
    rows, _, ring, c1 = xin_ref.shape
    own = ring - EDGE
    c2 = down_ref.shape[1]
    half = rows // 2
    place = Place(sizes, pieces)
    inside = place.column_mask(ring, own)

    def mask_to(extent):
        return lambda r: inside * place.above if r < 0 else inside * place.below if r >= extent else inside

    for n in range(HALO):
        put_planes(x_ref, n, top_ref[n, 0].astype(F32), top_ref[n, 1].astype(F32))
        put_planes(x_ref, HALO + n, bot_ref[n, 0].astype(F32), bot_ref[n, 1].astype(F32))

    def x_of(r):
        return (x_ref, r + HALO) if r < 0 else (xin_ref, r) if r < rows else (x_ref, HALO + r - rows)

    def h1_of(r):
        if 2 <= r < rows - 2:
            return h1in_ref, r - 2
        if -1 <= r < 2:
            return h1_ref, r + 1
        return (h1_ref, 3 + r - (rows - 2)) if rows - 2 <= r <= rows else None

    def ci_of(i):
        if 1 <= i < half - 1:
            return ciin_ref, i - 1
        return (ci_ref, i + 2) if i < 1 else (ci_ref, 3 + i - (half - 1))

    def h2_of(r):
        if 4 <= r < rows - 4:
            return h2in_ref, r - 4
        return (h2_ref, r + 1) if r < 4 else (h2_ref, 5 + r - (rows - 4))

    def h3_of(r):
        return (h3in_ref, r - 6) if 6 <= r < rows - 6 else (h3_ref, r) if r < 6 else (h3_ref, 6 + r - (rows - 6))

    pairs = [-2, -1, 0, half - 1, half, half + 1]
    first_conv(x_of, h1_of, pool_ref, pairs.index, pairs, w_ref.at[0], ring, c1)
    coarse_in(pool_ref, down_ref, ci_of, pairs, mask_to(half), ring, c2)
    order = [-1, 0, 1, half - 2, half - 1, half]
    coarse_conv(ci_of, co_ref, order, coarse_ref, ring)
    wanted = [r for r in range(-1, rows + 1) if not 4 <= r < rows - 4]
    lift(co_ref, up_ref, order, h1_of, h2_of, mask_to(rows), wanted, ring)
    second_conv(h2_of, h3_of, [i for i in range(half) if not 3 <= i < half - 3], w_ref.at[1], ring, own, c1)

    spread = jnp.transpose(jnp.broadcast_to(outp_ref[...].astype(F32), (128, c1)))
    lane = lax.broadcasted_iota(jnp.int32, (c1, 128), 1)
    pick = jnp.concatenate([jnp.where(lane == r, spread, 0.0).astype(BF16) for r in range(rows)], axis=0)
    parts = []
    for q in range(2):
        found = [h3_of(r) for r in range(rows)]
        parts.append(jnp.concatenate([ref[q, at] for ref, at in found], axis=1))
    sums = jnp.dot(jnp.concatenate(parts, axis=0), pick, preferred_element_type=F32)
    for q in range(2):
        flat_ref[pl.ds(q, own, stride=2), :] = sums[q * own : (q + 1) * own]
    network = jnp.transpose(flat_ref[...])[:rows]

    level = jnp.full((1, 128), now_ref[0], F32)
    after = jnp.full((1, 128), next_ref[0], F32)
    scale_in = 1.0 / jnp.sqrt(level * level + 1.0)
    scale_skip = (1.0 / (level * level + 1.0))[:, :1]
    scale_out = (level * scale_in)[:, :1]
    ratio = (after / level)[:, :1]
    spread_by = jnp.sqrt(level * level - after * after)[:, :1]
    here = pl.ds(pl.multiple_of(place.piece * 2 * own, 128), 2 * own)
    noisy = noisy_ref[:, here]
    denoised = scale_skip * noisy + scale_out * network
    out_ref[...] = denoised + ratio * (noisy - denoised) + spread_by * noise_ref[:, here]


def near(*arrays):
    return [pltpu.with_memory_space_constraint(a, pltpu.VMEM) for a in arrays]


def per_device(
    sizes,
    noisy_field, noise_draw, cond_features, sigma_now, sigma_next, field_proj,
    fine_kernels, coarse_kernel, down_proj, up_proj, out_proj,
):
    rows, cols, c1 = cond_features.shape
    c2 = down_proj.shape[1]
    patches, copies = sizes["patch"], sizes["fsdp"]
    pieces = 2 if copies % 2 == 0 and cols % 256 == 0 else 1
    if sizes["sub"] != 2 or rows < 16:
        raise ValueError("unsupported split")
    window = cols // pieces
    own = window // 2
    ring = own + EDGE
    half = rows // 2
    smem = pl.BlockSpec(memory_space=pltpu.SMEM)
    vmem = pl.BlockSpec(memory_space=pltpu.VMEM)
    where = dict(sizes=sizes, pieces=pieces)
    limit = lambda mib: pltpu.CompilerParams(vmem_limit_bytes=mib << 20)

    mine, tile, send = pl.pallas_call(
        functools.partial(embed_kernel, **where),
        out_shape=[
            pltpu.VMEM((rows, 2, own, c1), BF16),
            pltpu.VMEM((rows, 2, EDGE, c1), BF16),
            pltpu.VMEM((rows, 2, PER, c1), BF16),
        ],
        in_specs=[smem] + [pl.BlockSpec(memory_space=pltpu.HBM)] * 3,
        out_specs=[vmem] * 3,
        scratch_shapes=[
            pltpu.VMEM((rows, window, c1), BF16),
            pltpu.VMEM((rows, EDGE, c1), BF16),
            pltpu.VMEM((rows, EDGE, c1), BF16),
            pltpu.VMEM((rows, cols), F32),
            pltpu.VMEM((1, c1), F32),
            pltpu.VMEM((cols, 128), F32),
            pltpu.VMEM((2, window, c1), F32),
            pltpu.VMEM((2, 2 * EDGE, c1), F32),
            pltpu.SemaphoreType.DMA((5,)),
        ],
        compiler_params=limit(8),
        name="embed",
    )(sigma_now, *[pltpu.with_memory_space_constraint(a, pltpu.HBM) for a in (cond_features, noisy_field, field_proj[None])])

    got = lax.ppermute(send, "sub", [(0, 1), (1, 0)])

    full, upward, downward = pl.pallas_call(
        functools.partial(border_kernel, **where),
        out_shape=[
            pltpu.VMEM((rows, 2, EDGE, c1), BF16),
            pltpu.VMEM((HALO, 2, ring, c1), BF16),
            pltpu.VMEM((HALO, 2, ring, c1), BF16),
        ],
        in_specs=[vmem] * 3,
        out_specs=[vmem] * 3,
        compiler_params=limit(4),
        name="border",
    )(*near(mine, tile, got))

    top = lax.ppermute(upward, "patch", [(i, i + 1) for i in range(patches - 1)])
    bot = lax.ppermute(downward, "patch", [(i + 1, i) for i in range(patches - 1)])

    weights = near(coarse_kernel.reshape(9 * c2, c2), down_proj, up_proj)
    work = 2 * ring * c1 * c1 * 18 * 2 * (half - 2) + 2 * ring * 9 * c2 * c2 * (half - 4)
    inner = pl.pallas_call(
        functools.partial(inner_kernel, **where),
        out_shape=[
            pltpu.VMEM((rows, 4, ring, c1), BF16),
            pltpu.VMEM((2, 12 * c1, 2 * c1), BF16),
            pltpu.VMEM((rows - 4, 2, ring, c1), BF16),
            pltpu.VMEM((half - 2, 3, ring, c2), BF16),
            pltpu.VMEM((rows - 8, 4, ring, c1), BF16),
            pltpu.VMEM((2, rows - 12, own, c1), BF16),
        ],
        in_specs=[vmem] * 6,
        out_specs=[vmem] * 6,
        scratch_shapes=[
            pltpu.VMEM(((half - 2) * ring, c1), BF16),
            pltpu.VMEM(((half - 4) * ring, c2), BF16),
        ],
        cost_estimate=pl.CostEstimate(flops=work * 2, bytes_accessed=4 << 20, transcendentals=0),
        compiler_params=limit(12),
        name="inner",
    )(*near(mine, full, fine_kernels), *weights)

    part = pl.pallas_call(
        functools.partial(outer_kernel, **where),
        out_shape=pltpu.VMEM((rows, window), F32),
        in_specs=[smem, smem] + [vmem] * 14,
        out_specs=vmem,
        scratch_shapes=[
            pltpu.VMEM((2 * HALO, 4, ring, c1), BF16),
            pltpu.VMEM((6 * ring, c1), BF16),
            pltpu.VMEM((6, 2, ring, c1), BF16),
            pltpu.VMEM((6, 3, ring, c2), BF16),
            pltpu.VMEM((6 * ring, c2), BF16),
            pltpu.VMEM((10, 4, ring, c1), BF16),
            pltpu.VMEM((2, 12, own, c1), BF16),
            pltpu.VMEM((window, 128), F32),
        ],
        compiler_params=limit(16),
        name="outer",
    )(sigma_now, sigma_next, *near(top, bot, *inner), *weights, *near(out_proj[None], noisy_field, noise_draw))
    if pieces == 1:
        return part
    other = lax.ppermute(part, "fsdp", [(i, i ^ 1) for i in range(copies)])
    first = lax.rem(lax.axis_index("fsdp"), pieces) == 0
    return jnp.where(first, jnp.concatenate([part, other], axis=1), jnp.concatenate([other, part], axis=1))


def solution(mesh):
    return jax.shard_map(
        functools.partial(per_device, dict(mesh.shape)),
        mesh=mesh,
        in_specs=(
            P(("groups", "patch"), "sub"),
            P(("groups", "patch"), "sub"),
            P(("groups", "patch"), "sub", None),
            P(),
            P(),
            P(),
            P(),
            P(),
            P(),
            P(),
            P(),
        ),
        out_specs=P(("groups", "patch"), "sub"),
        check_vma=False,
    )
```

```python
import functools

import jax
import jax.numpy as jnp
from jax import lax
from jax.experimental import pallas as pl
from jax.experimental.pallas import tpu as pltpu
from jax.sharding import PartitionSpec as P

F32 = jnp.float32
BF16 = jnp.bfloat16
HALO = 5
EDGE = 16
PER = EDGE // 2
CHUNK = 3


def silu(v):
    half = 0.5 * v
    return half + half * jnp.tanh(half)


def flag(condition):
    return jnp.where(condition, 1.0, 0.0).astype(F32)


class Place:
    def __init__(self, sizes, pieces):
        self.piece = lax.rem(lax.axis_index("fsdp"), pieces)
        self.sub = lax.axis_index("sub")
        self.patch = lax.axis_index("patch")
        self.first = self.piece == 0
        self.last = self.piece == pieces - 1
        self.has_left = jnp.logical_or(self.piece > 0, self.sub > 0)
        self.has_right = jnp.logical_or(self.piece < pieces - 1, self.sub < sizes["sub"] - 1)
        self.above = flag(self.patch > 0)
        self.below = flag(self.patch < sizes["patch"] - 1)

    def column_mask(self, ring, own):
        at = lax.broadcasted_iota(jnp.int32, (ring, 128), 0)
        return jnp.where(at < own, 1.0, jnp.where(at < own + PER, flag(self.has_right), flag(self.has_left)))


def embed_kernel(
    now_ref, cond_ref, noisy_ref, proj_ref, mine_ref, tile_ref, send_ref,
    main, inner, give, field, embedding, turned, wide, edge, sems, *, sizes, pieces,
):
    rows, window, _ = main.shape
    cols = noisy_ref.shape[1]
    place = Place(sizes, pieces)
    start = pl.multiple_of(place.piece * window, EDGE)
    near_by = pl.multiple_of(jnp.where(place.first, window, start - EDGE), EDGE)
    given = pl.multiple_of(jnp.where(place.sub == 0, cols - EDGE, 0), EDGE)
    small = [
        pltpu.make_async_copy(noisy_ref, field, sems.at[3]),
        pltpu.make_async_copy(proj_ref, embedding, sems.at[4]),
    ]
    copies = [pltpu.make_async_copy(cond_ref.at[:, pl.ds(given, EDGE)], give, sems.at[0])]
    if pieces > 1:
        copies.append(pltpu.make_async_copy(cond_ref.at[:, pl.ds(near_by, EDGE)], inner, sems.at[1]))
    copies.append(pltpu.make_async_copy(cond_ref.at[:, pl.ds(start, window)], main, sems.at[2]))
    for copy in small + copies:
        copy.start()
    for copy in small:
        copy.wait()
    level = now_ref[...]
    scale_in = 1.0 / jnp.sqrt(level * level + 1.0)
    turned[:, :rows] = jnp.transpose(field[...] * scale_in)
    proj = embedding[...]

    def hidden(buf, r, at):
        return buf[r].astype(F32) + turned[pl.ds(at, buf.shape[1]), r : r + 1] * proj

    for copy in copies[:-1]:
        copy.wait()
    for r in range(rows):
        edge[r % 2, :EDGE] = hidden(give, r, given)
        for q in range(2):
            send_ref[r, q] = edge[r % 2, pl.ds(q, PER, stride=2), :].astype(BF16)
        if pieces > 1:
            edge[r % 2, EDGE:] = hidden(inner, r, near_by)
            for q in range(2):
                block = edge[r % 2, pl.ds(EDGE + q, PER, stride=2), :]
                to_right = block * flag(jnp.logical_not(place.last))
                to_left = block * flag(jnp.logical_not(place.first))
                tile_ref[r, q] = jnp.concatenate([to_right, to_left], axis=0).astype(BF16)
        else:
            tile_ref[r] = jnp.zeros_like(tile_ref[r])
    copies[-1].wait()
    for r in range(rows):
        wide[r % 2] = hidden(main, r, start)
        for q in range(2):
            mine_ref[r, q] = wide[r % 2, pl.ds(q, window // 2, stride=2), :].astype(BF16)


def border_kernel(mine_ref, tile_ref, got_ref, full_ref, even_ref, odd_ref, brief, *, sizes, pieces):
    rows, _, own, _ = mine_ref.shape
    place = Place(sizes, pieces)
    right = flag(jnp.logical_and(place.last, place.has_right))
    left = flag(jnp.logical_and(place.first, place.has_left))
    head = lax.broadcasted_iota(jnp.int32, (PER, 128), 0) < PER // 2
    for r in range(rows):
        for q in range(2):
            got = got_ref[r, q].astype(F32)
            tile = tile_ref[r, q].astype(F32) + jnp.concatenate([got * right, got * left], axis=0)
            full_ref[r, q] = tile.astype(BF16)
            brief[r, q] = jnp.where(head, tile[:PER], tile[PER:]).astype(BF16)
    low = lax.rem(place.patch, 2) == 0
    for ref, start in ((even_ref, jnp.where(low, rows - HALO, 0)), (odd_ref, jnp.where(low, 0, rows - HALO))):
        for n in range(HALO):
            ref[n, :, :own] = mine_ref[start + n]
            ref[n, :, own:] = brief[start + n]


def put_planes(ref, at, even, odd):
    ring = even.shape[0]
    ref[at, 0] = even.astype(BF16)
    ref[at, 1] = odd.astype(BF16)
    ref[at, 2] = pltpu.roll(odd, 1, 0).astype(BF16)
    ref[at, 3] = pltpu.roll(even, ring - 1, 0).astype(BF16)


def chunks(rows_of):
    return [rows_of[k : k + CHUNK] for k in range(0, len(rows_of), CHUNK)]


def conv_pairs(planes_of, pairs, weight, kept):
    parts = []
    for i in pairs:
        found = [planes_of(2 * i - 1 + d) for d in range(4)]
        for planes in ((2, 0, 1), (0, 1, 3)):
            parts.append(jnp.concatenate([ref[at, k, :kept] for k in planes for ref, at in found], axis=1))
    return jnp.dot(jnp.concatenate(parts, axis=0), weight[...], preferred_element_type=F32)


def first_conv(planes_of, h1_of, pool_ref, slot_of, pairs, weight, ring, c1):
    for group in chunks(pairs):
        acc = conv_pairs(planes_of, group, weight, ring)
        for n, i in enumerate(group):
            total = None
            for o in range(2):
                ref, at = planes_of(2 * i + o)
                for q in range(2):
                    v = acc[(2 * n + q) * ring : (2 * n + q + 1) * ring, o * c1 : (o + 1) * c1]
                    h = (ref[at, q].astype(F32) + silu(v)).astype(BF16)
                    kept = h1_of(2 * i + o)
                    if kept is not None:
                        kept[0][kept[1], q] = h
                    total = h.astype(F32) if total is None else total + h.astype(F32)
            pool_ref[slot_of(i) * ring : (slot_of(i) + 1) * ring] = (total * 0.25).astype(BF16)


def coarse_in(pool_ref, down_ref, ci_of, order, mask_of, ring, c2):
    ci_all = jnp.dot(pool_ref[...], down_ref[...], preferred_element_type=F32)
    for n, i in enumerate(order):
        ci = ci_all[n * ring : (n + 1) * ring] * jnp.concatenate([mask_of(i)] * (c2 // 128), axis=1)
        ref, at = ci_of(i)
        ref[at, 0] = pltpu.roll(ci, 1, 0).astype(BF16)
        ref[at, 1] = ci.astype(BF16)
        ref[at, 2] = pltpu.roll(ci, ring - 1, 0).astype(BF16)


def coarse_conv(ci_of, co_ref, order, coarse_ref, ring):
    for k, group in enumerate(chunks(order)):
        parts = []
        for i in group:
            found = [ci_of(i - 1 + a) for a in range(3)]
            parts.append(jnp.concatenate([ref[at, b] for ref, at in found for b in range(3)], axis=1))
        v = jnp.dot(jnp.concatenate(parts, axis=0), coarse_ref[...], preferred_element_type=F32)
        for n, i in enumerate(group):
            ref, at = ci_of(i)
            slot = k * CHUNK + n
            co = ref[at, 1].astype(F32) + silu(v[n * ring : (n + 1) * ring])
            co_ref[slot * ring : (slot + 1) * ring] = co.astype(BF16)


def lift(co_ref, up_ref, order, h1_of, h2_of, mask_of, wanted, ring):
    lifted_all = jnp.dot(co_ref[...], up_ref[...], preferred_element_type=F32)
    for n, i in enumerate(order):
        lifted = lifted_all[n * ring : (n + 1) * ring]
        for r in (2 * i, 2 * i + 1):
            if r in wanted:
                ref, at = h1_of(r)
                mask = mask_of(r)
                into, slot = h2_of(r)
                put_planes(into, slot, (ref[at, 0].astype(F32) + lifted) * mask, (ref[at, 1].astype(F32) + lifted) * mask)


def second_conv(h2_of, h3_of, pairs, weight, own, c1):
    for group in chunks(pairs):
        acc = conv_pairs(h2_of, group, weight, own)
        for n, i in enumerate(group):
            for o in range(2):
                ref, at = h2_of(2 * i + o)
                into, slot = h3_of(2 * i + o)
                for q in range(2):
                    v = acc[(2 * n + q) * own : (2 * n + q + 1) * own, o * c1 : (o + 1) * c1]
                    into[q, slot] = (ref[at, q, :own].astype(F32) + silu(v)).astype(BF16)


def pack_kernel(fine_ref, w_ref):
    c1 = fine_ref.shape[3]
    for layer in range(2):
        for b in range(3):
            for d in range(4):
                at = (b * 4 + d) * c1
                for o in range(2):
                    a = d - o
                    block = fine_ref[layer, a * 3 + b] if 0 <= a <= 2 else jnp.zeros((c1, c1), BF16)
                    w_ref[layer, at : at + c1, o * c1 : (o + 1) * c1] = block


def inner_kernel(
    mine_ref, tile_ref, w_ref, coarse_ref, down_ref, up_ref,
    x_ref, h1_ref, ci_ref, h2_ref, h3_ref, pool_ref, co_ref, *, sizes, pieces,
):
    rows, _, own, c1 = mine_ref.shape
    ring = own + EDGE
    c2 = down_ref.shape[1]
    half = rows // 2
    mask = Place(sizes, pieces).column_mask(ring, own)
    for r in range(rows):
        even, odd = (jnp.concatenate([mine_ref[r, q].astype(F32), tile_ref[r, q].astype(F32)], axis=0) for q in range(2))
        put_planes(x_ref, r, even, odd)
    x_of = lambda r: (x_ref, r)
    h1_of = lambda r: (h1_ref, r - 2)
    ci_of = lambda i: (ci_ref, i - 1)
    h2_of = lambda r: (h2_ref, r - 4)
    h3_of = lambda r: (h3_ref, r - 6)
    first_conv(x_of, h1_of, pool_ref, lambda i: i - 1, list(range(1, half - 1)), w_ref.at[0], ring, c1)
    coarse_in(pool_ref, down_ref, ci_of, range(1, half - 1), lambda i: mask, ring, c2)
    coarse_conv(ci_of, co_ref, list(range(2, half - 2)), coarse_ref, ring)
    lift(co_ref, up_ref, range(2, half - 2), h1_of, h2_of, lambda r: mask, range(4, rows - 4), ring)
    second_conv(h2_of, h3_of, list(range(3, half - 3)), w_ref.at[1], own, c1)


def outer_kernel(
    now_ref, next_ref, odd_ref, even_ref, xin_ref, w_ref, h1in_ref, ciin_ref, h2in_ref, h3in_ref,
    coarse_ref, down_ref, up_ref, outp_ref, noisy_ref, noise_ref, out_ref,
    x_ref, pool_ref, h1_ref, ci_ref, co_ref, h2_ref, h3_ref, flat_ref, *, sizes, pieces,
):
    rows, _, ring, c1 = xin_ref.shape
    own = ring - EDGE
    c2 = down_ref.shape[1]
    half = rows // 2
    place = Place(sizes, pieces)
    inside = place.column_mask(ring, own)

    def mask_to(extent):
        return lambda r: inside * place.above if r < 0 else inside * place.below if r >= extent else inside

    low = lax.rem(place.patch, 2) == 0
    head = lax.broadcasted_iota(jnp.int32, (PER, 128), 0) < PER // 2
    for n in range(HALO):
        above, below = [], []
        for q in range(2):
            by_odd, by_even = odd_ref[n, q].astype(F32), even_ref[n, q].astype(F32)
            for into, v in ((above, jnp.where(low, by_odd, by_even)), (below, jnp.where(low, by_even, by_odd))):
                edge = v[own:]
                into.append(jnp.concatenate([v[:own], jnp.where(head, edge, 0.0), jnp.where(head, 0.0, edge)], axis=0))
        put_planes(x_ref, n, *above)
        put_planes(x_ref, HALO + n, *below)

    def x_of(r):
        return (x_ref, r + HALO) if r < 0 else (xin_ref, r) if r < rows else (x_ref, HALO + r - rows)

    def h1_of(r):
        if 2 <= r < rows - 2:
            return h1in_ref, r - 2
        if -1 <= r < 2:
            return h1_ref, r + 1
        return (h1_ref, 3 + r - (rows - 2)) if rows - 2 <= r <= rows else None

    def ci_of(i):
        if 1 <= i < half - 1:
            return ciin_ref, i - 1
        return (ci_ref, i + 2) if i < 1 else (ci_ref, 3 + i - (half - 1))

    def h2_of(r):
        if 4 <= r < rows - 4:
            return h2in_ref, r - 4
        return (h2_ref, r + 1) if r < 4 else (h2_ref, 5 + r - (rows - 4))

    def h3_of(r):
        return (h3in_ref, r - 6) if 6 <= r < rows - 6 else (h3_ref, r) if r < 6 else (h3_ref, 6 + r - (rows - 6))

    pairs = [-2, -1, 0, half - 1, half, half + 1]
    first_conv(x_of, h1_of, pool_ref, pairs.index, pairs, w_ref.at[0], ring, c1)
    coarse_in(pool_ref, down_ref, ci_of, pairs, mask_to(half), ring, c2)
    order = [-1, 0, 1, half - 2, half - 1, half]
    coarse_conv(ci_of, co_ref, order, coarse_ref, ring)
    wanted = [r for r in range(-1, rows + 1) if not 4 <= r < rows - 4]
    lift(co_ref, up_ref, order, h1_of, h2_of, mask_to(rows), wanted, ring)
    second_conv(h2_of, h3_of, [i for i in range(half) if not 3 <= i < half - 3], w_ref.at[1], own, c1)

    spread = jnp.transpose(jnp.broadcast_to(outp_ref[...].astype(F32), (128, c1)))
    lane = lax.broadcasted_iota(jnp.int32, (c1, 128), 1)
    pick = jnp.concatenate([jnp.where(lane == r, spread, 0.0).astype(BF16) for r in range(rows)], axis=0)
    parts = []
    for q in range(2):
        found = [h3_of(r) for r in range(rows)]
        parts.append(jnp.concatenate([ref[q, at] for ref, at in found], axis=1))
    sums = jnp.dot(jnp.concatenate(parts, axis=0), pick, preferred_element_type=F32)
    for q in range(2):
        flat_ref[pl.ds(q, own, stride=2), :] = sums[q * own : (q + 1) * own]
    network = jnp.transpose(flat_ref[...])[:rows]

    level = now_ref[...]
    after = next_ref[...]
    scale_in = 1.0 / jnp.sqrt(level * level + 1.0)
    scale_skip = 1.0 / (level * level + 1.0)
    scale_out = level * scale_in
    ratio = after / level
    spread_by = jnp.sqrt(level * level - after * after)
    here = pl.ds(pl.multiple_of(place.piece * 2 * own, 128), 2 * own)
    noisy = noisy_ref[:, here]
    denoised = scale_skip * noisy + scale_out * network
    out_ref[...] = denoised + ratio * (noisy - denoised) + spread_by * noise_ref[:, here]


def near(*arrays):
    return [pltpu.with_memory_space_constraint(a, pltpu.VMEM) for a in arrays]


def per_device(
    sizes,
    noisy_field, noise_draw, cond_features, sigma_now, sigma_next, field_proj,
    fine_kernels, coarse_kernel, down_proj, up_proj, out_proj,
):
    rows, cols, c1 = cond_features.shape
    c2 = down_proj.shape[1]
    patches, copies = sizes["patch"], sizes["fsdp"]
    pieces = 2 if copies % 2 == 0 and cols % 256 == 0 else 1
    if sizes["sub"] != 2 or rows < 16:
        raise ValueError("unsupported split")
    window = cols // pieces
    own = window // 2
    ring = own + EDGE
    half = rows // 2
    vmem = pl.BlockSpec(memory_space=pltpu.VMEM)
    where = dict(sizes=sizes, pieces=pieces)
    limit = lambda mib: pltpu.CompilerParams(vmem_limit_bytes=mib << 20)

    mine, tile, send = pl.pallas_call(
        functools.partial(embed_kernel, **where),
        out_shape=[
            pltpu.VMEM((rows, 2, own, c1), BF16),
            pltpu.VMEM((rows, 2, EDGE, c1), BF16),
            pltpu.VMEM((rows, 2, PER, c1), BF16),
        ],
        in_specs=[vmem] + [pl.BlockSpec(memory_space=pltpu.HBM)] * 3,
        out_specs=[vmem] * 3,
        scratch_shapes=[
            pltpu.VMEM((rows, window, c1), BF16),
            pltpu.VMEM((rows, EDGE, c1), BF16),
            pltpu.VMEM((rows, EDGE, c1), BF16),
            pltpu.VMEM((rows, cols), F32),
            pltpu.VMEM((1, c1), F32),
            pltpu.VMEM((cols, 128), F32),
            pltpu.VMEM((2, window, c1), F32),
            pltpu.VMEM((2, 2 * EDGE, c1), F32),
            pltpu.SemaphoreType.DMA((5,)),
        ],
        compiler_params=limit(8),
        name="embed",
    )(sigma_now[None], *[pltpu.with_memory_space_constraint(a, pltpu.HBM) for a in (cond_features, noisy_field, field_proj[None])])

    got = lax.ppermute(send, "sub", [(0, 1), (1, 0)])

    packed = pl.pallas_call(
        pack_kernel,
        out_shape=pltpu.VMEM((2, 12 * c1, 2 * c1), BF16),
        in_specs=[vmem],
        out_specs=vmem,
        cost_estimate=pl.CostEstimate(flops=0, bytes_accessed=2 << 20, transcendentals=0),
        compiler_params=limit(4),
        name="pack",
    )(*near(fine_kernels))

    full, for_even, for_odd = pl.pallas_call(
        functools.partial(border_kernel, **where),
        out_shape=[
            pltpu.VMEM((rows, 2, EDGE, c1), BF16),
            pltpu.VMEM((HALO, 2, own + PER, c1), BF16),
            pltpu.VMEM((HALO, 2, own + PER, c1), BF16),
        ],
        in_specs=[vmem] * 3,
        out_specs=[vmem] * 3,
        scratch_shapes=[pltpu.VMEM((rows, 2, PER, c1), BF16)],
        compiler_params=limit(4),
        name="border",
    )(*near(mine, tile, got))

    def swap(rows_to_give, low):
        return lax.ppermute(rows_to_give, "patch", [pair for i in range(low, patches - 1, 2) for pair in ((i, i + 1), (i + 1, i))])

    odd = swap(for_odd, 1)
    even = swap(for_even, 0)

    weights = near(coarse_kernel.reshape(9 * c2, c2), down_proj, up_proj)
    work = 2 * ring * c1 * c1 * 18 * 2 * (half - 2) + 2 * ring * 9 * c2 * c2 * (half - 4)
    inner = pl.pallas_call(
        functools.partial(inner_kernel, **where),
        out_shape=[
            pltpu.VMEM((rows, 4, ring, c1), BF16),
            pltpu.VMEM((rows - 4, 2, ring, c1), BF16),
            pltpu.VMEM((half - 2, 3, ring, c2), BF16),
            pltpu.VMEM((rows - 8, 4, ring, c1), BF16),
            pltpu.VMEM((2, rows - 12, own, c1), BF16),
        ],
        in_specs=[vmem] * 6,
        out_specs=[vmem] * 5,
        scratch_shapes=[
            pltpu.VMEM(((half - 2) * ring, c1), BF16),
            pltpu.VMEM(((half - 4) * ring, c2), BF16),
        ],
        cost_estimate=pl.CostEstimate(flops=work * 2, bytes_accessed=4 << 20, transcendentals=0),
        compiler_params=limit(12),
        name="inner",
    )(*near(mine, full, packed), *weights)

    part = pl.pallas_call(
        functools.partial(outer_kernel, **where),
        out_shape=pltpu.VMEM((rows, window), F32),
        in_specs=[vmem] * 16,
        out_specs=vmem,
        scratch_shapes=[
            pltpu.VMEM((2 * HALO, 4, ring, c1), BF16),
            pltpu.VMEM((6 * ring, c1), BF16),
            pltpu.VMEM((6, 2, ring, c1), BF16),
            pltpu.VMEM((6, 3, ring, c2), BF16),
            pltpu.VMEM((6 * ring, c2), BF16),
            pltpu.VMEM((10, 4, ring, c1), BF16),
            pltpu.VMEM((2, 12, own, c1), BF16),
            pltpu.VMEM((window, 128), F32),
        ],
        compiler_params=limit(16),
        name="outer",
    )(sigma_now[None], sigma_next[None], *near(odd, even, *inner[:1], packed, *inner[1:]), *weights, *near(out_proj[None], noisy_field, noise_draw))
    if pieces == 1:
        return part
    other = lax.ppermute(part, "fsdp", [(i, i ^ 1) for i in range(copies)])
    first = lax.rem(lax.axis_index("fsdp"), pieces) == 0
    return jnp.where(first, jnp.concatenate([part, other], axis=1), jnp.concatenate([other, part], axis=1))


def solution(mesh):
    return jax.shard_map(
        functools.partial(per_device, dict(mesh.shape)),
        mesh=mesh,
        in_specs=(
            P(("groups", "patch"), "sub"),
            P(("groups", "patch"), "sub"),
            P(("groups", "patch"), "sub", None),
            P(),
            P(),
            P(),
            P(),
            P(),
            P(),
            P(),
            P(),
        ),
        out_specs=P(("groups", "patch"), "sub"),
        check_vma=False,
    )
```

```python
import functools

import jax
import jax.numpy as jnp
from jax import lax
from jax.experimental import pallas as pl
from jax.experimental.pallas import tpu as pltpu
from jax.sharding import PartitionSpec as P

F32 = jnp.float32
BF16 = jnp.bfloat16
HALO = 5
EDGE = 16
PER = EDGE // 2
CHUNK = 3


def silu_of_half(half):
    return half + half * jnp.tanh(half)


def silu(v):
    return silu_of_half(0.5 * v)


def flag(condition):
    return jnp.where(condition, 1.0, 0.0).astype(F32)


class Place:
    def __init__(self, sizes, pieces):
        self.piece = lax.rem(lax.axis_index("fsdp"), pieces)
        self.sub = lax.axis_index("sub")
        self.patch = lax.axis_index("patch")
        self.first = self.piece == 0
        self.last = self.piece == pieces - 1
        self.has_left = jnp.logical_or(self.piece > 0, self.sub > 0)
        self.has_right = jnp.logical_or(self.piece < pieces - 1, self.sub < sizes["sub"] - 1)
        self.above = flag(self.patch > 0)
        self.below = flag(self.patch < sizes["patch"] - 1)

    def column_mask(self, ring, own):
        at = lax.broadcasted_iota(jnp.int32, (ring, 128), 0)
        return jnp.where(at < own, 1.0, jnp.where(at < own + PER // 2, flag(self.has_right), flag(self.has_left)))


def embed_kernel(
    now_ref, cond_ref, noisy_ref, proj_ref, mine_ref, tile_ref, send_ref,
    main, inner, give, field, embedding, turned, wide, edge, sems, *, sizes, pieces,
):
    rows, window, _ = main.shape
    cols = noisy_ref.shape[1]
    place = Place(sizes, pieces)
    start = pl.multiple_of(place.piece * window, EDGE)
    near_by = pl.multiple_of(jnp.where(place.first, window, start - EDGE), EDGE)
    given = pl.multiple_of(jnp.where(place.sub == 0, cols - EDGE, 0), EDGE)
    small = [
        pltpu.make_async_copy(noisy_ref, field, sems.at[3]),
        pltpu.make_async_copy(proj_ref, embedding, sems.at[4]),
    ]
    copies = [pltpu.make_async_copy(cond_ref.at[:, pl.ds(given, EDGE)], give, sems.at[0])]
    if pieces > 1:
        copies.append(pltpu.make_async_copy(cond_ref.at[:, pl.ds(near_by, EDGE)], inner, sems.at[1]))
    copies.append(pltpu.make_async_copy(cond_ref.at[:, pl.ds(start, window)], main, sems.at[2]))
    for copy in small + copies:
        copy.start()
    for copy in small:
        copy.wait()
    level = now_ref[...]
    scale_in = 1.0 / jnp.sqrt(level * level + 1.0)
    turned[:, :rows] = jnp.transpose(field[...] * scale_in)
    proj = embedding[...]
    head = lax.broadcasted_iota(jnp.int32, (PER, 128), 0) < PER // 2

    def hidden(buf, r, at):
        return buf[r].astype(F32) + turned[pl.ds(at, buf.shape[1]), r : r + 1] * proj

    for copy in copies[:-1]:
        copy.wait()
    for r in range(rows):
        edge[r % 2, :EDGE] = hidden(give, r, given)
        for q in range(2):
            send_ref[r, q] = edge[r % 2, pl.ds(q, PER, stride=2), :].astype(BF16)
        if pieces > 1:
            edge[r % 2, EDGE:] = hidden(inner, r, near_by)
            for q in range(2):
                block = edge[r % 2, pl.ds(EDGE + q, PER, stride=2), :]
                to_right = block * flag(jnp.logical_not(place.last))
                to_left = block * flag(jnp.logical_not(place.first))
                tile_ref[r, q] = jnp.where(head, to_right, to_left).astype(BF16)
        else:
            tile_ref[r] = jnp.zeros_like(tile_ref[r])
    copies[-1].wait()
    for r in range(rows):
        wide[r % 2] = hidden(main, r, start)
        for q in range(2):
            mine_ref[r, q] = wide[r % 2, pl.ds(q, window // 2, stride=2), :].astype(BF16)


def border_kernel(mine_ref, tile_ref, got_ref, full_ref, even_ref, odd_ref, *, sizes, pieces):
    rows, _, own, _ = mine_ref.shape
    place = Place(sizes, pieces)
    right = flag(jnp.logical_and(place.last, place.has_right))
    left = flag(jnp.logical_and(place.first, place.has_left))
    head = lax.broadcasted_iota(jnp.int32, (PER, 128), 0) < PER // 2
    for r in range(rows):
        for q in range(2):
            got = got_ref[r, q].astype(F32)
            tile = tile_ref[r, q].astype(F32) + jnp.where(head, got * right, got * left)
            full_ref[r, q] = tile.astype(BF16)
    low = lax.rem(place.patch, 2) == 0
    for ref, start in ((even_ref, jnp.where(low, rows - HALO, 0)), (odd_ref, jnp.where(low, 0, rows - HALO))):
        for n in range(HALO):
            ref[n, :, :own] = mine_ref[start + n]
            ref[n, :, own:] = full_ref[start + n]


def put_planes(ref, at, even, odd):
    ring = even.shape[0]
    ref[at, 0] = even.astype(BF16)
    ref[at, 1] = odd.astype(BF16)
    ref[at, 2] = pltpu.roll(odd, 1, 0).astype(BF16)
    ref[at, 3] = pltpu.roll(even, ring - 1, 0).astype(BF16)


def masked(x, columns, row):
    own = x.shape[0] - PER
    columns = jnp.concatenate([columns[own:]] * (x.shape[1] // 128), axis=1)
    x = jnp.concatenate([x[:own], x[own:] * columns], axis=0)
    return x if row is None else x * row


def chunks(rows_of):
    return [rows_of[k : k + CHUNK] for k in range(0, len(rows_of), CHUNK)]


def conv_pairs(planes_of, pairs, weight, kept):
    parts = []
    for i in pairs:
        found = [planes_of(2 * i - 1 + d) for d in range(4)]
        for planes in ((2, 0, 1), (0, 1, 3)):
            parts.append(jnp.concatenate([ref[at, k, :kept] for k in planes for ref, at in found], axis=1))
    return jnp.dot(jnp.concatenate(parts, axis=0), weight[...], preferred_element_type=F32)


def first_conv(planes_of, h1_of, pool_ref, slot_of, pairs, weight, ring, c1):
    for group in chunks(pairs):
        acc = conv_pairs(planes_of, group, weight, ring)
        for n, i in enumerate(group):
            total = None
            for o in range(2):
                ref, at = planes_of(2 * i + o)
                for q in range(2):
                    v = acc[(2 * n + q) * ring : (2 * n + q + 1) * ring, o * c1 : (o + 1) * c1]
                    h = (ref[at, q].astype(F32) + silu_of_half(v)).astype(BF16)
                    kept = h1_of(2 * i + o)
                    if kept is not None:
                        kept[0][kept[1], q] = h
                    total = h.astype(F32) if total is None else total + h.astype(F32)
            pool_ref[slot_of(i) * ring : (slot_of(i) + 1) * ring] = (total * 0.25).astype(BF16)


def coarse_in(pool_ref, down_ref, ci_of, order, mask_of, ring, c2):
    ci_all = jnp.dot(pool_ref[...], down_ref[...], preferred_element_type=F32)
    for n, i in enumerate(order):
        ci = masked(ci_all[n * ring : (n + 1) * ring], *mask_of(i))
        ref, at = ci_of(i)
        ref[at, 0] = pltpu.roll(ci, 1, 0).astype(BF16)
        ref[at, 1] = ci.astype(BF16)
        ref[at, 2] = pltpu.roll(ci, ring - 1, 0).astype(BF16)


def coarse_conv(ci_of, co_ref, order, coarse_ref, ring):
    for k, group in enumerate(chunks(order)):
        parts = []
        for i in group:
            found = [ci_of(i - 1 + a) for a in range(3)]
            parts.append(jnp.concatenate([ref[at, b] for ref, at in found for b in range(3)], axis=1))
        v = jnp.dot(jnp.concatenate(parts, axis=0), coarse_ref[...], preferred_element_type=F32)
        for n, i in enumerate(group):
            ref, at = ci_of(i)
            slot = k * CHUNK + n
            co = ref[at, 1].astype(F32) + silu(v[n * ring : (n + 1) * ring])
            co_ref[slot * ring : (slot + 1) * ring] = co.astype(BF16)


def lift(co_ref, up_ref, order, h1_of, h2_of, mask_of, wanted, ring):
    lifted_all = jnp.dot(co_ref[...], up_ref[...], preferred_element_type=F32)
    for n, i in enumerate(order):
        lifted = lifted_all[n * ring : (n + 1) * ring]
        for r in (2 * i, 2 * i + 1):
            if r in wanted:
                ref, at = h1_of(r)
                mask = mask_of(r)
                into, slot = h2_of(r)
                put_planes(into, slot, *(masked(ref[at, q].astype(F32) + lifted, *mask) for q in range(2)))


def second_conv(h2_of, h3_of, pairs, weight, own, c1):
    for group in chunks(pairs):
        acc = conv_pairs(h2_of, group, weight, own)
        for n, i in enumerate(group):
            for o in range(2):
                ref, at = h2_of(2 * i + o)
                into, slot = h3_of(2 * i + o)
                for q in range(2):
                    v = acc[(2 * n + q) * own : (2 * n + q + 1) * own, o * c1 : (o + 1) * c1]
                    into[q, slot] = (ref[at, q, :own].astype(F32) + silu_of_half(v)).astype(BF16)


def pack_kernel(fine_ref, w_ref):
    c1 = fine_ref.shape[3]
    for layer in range(2):
        for b in range(3):
            for d in range(4):
                at = (b * 4 + d) * c1
                for o in range(2):
                    a = d - o
                    block = fine_ref[layer, a * 3 + b] * 0.5 if 0 <= a <= 2 else jnp.zeros((c1, c1), BF16)
                    w_ref[layer, at : at + c1, o * c1 : (o + 1) * c1] = block


def inner_kernel(
    mine_ref, tile_ref, w_ref, coarse_ref, down_ref, up_ref,
    x_ref, h1_ref, ci_ref, h2_ref, h3_ref, pool_ref, co_ref, *, sizes, pieces,
):
    rows, _, own, c1 = mine_ref.shape
    ring = own + PER
    c2 = down_ref.shape[1]
    half = rows // 2
    mask = Place(sizes, pieces).column_mask(ring, own)
    for r in range(rows):
        even, odd = (jnp.concatenate([mine_ref[r, q].astype(F32), tile_ref[r, q].astype(F32)], axis=0) for q in range(2))
        put_planes(x_ref, r, even, odd)
    x_of = lambda r: (x_ref, r)
    h1_of = lambda r: (h1_ref, r - 2)
    ci_of = lambda i: (ci_ref, i - 1)
    h2_of = lambda r: (h2_ref, r - 4)
    h3_of = lambda r: (h3_ref, r - 6)
    first_conv(x_of, h1_of, pool_ref, lambda i: i - 1, list(range(1, half - 1)), w_ref.at[0], ring, c1)
    coarse_in(pool_ref, down_ref, ci_of, range(1, half - 1), lambda i: (mask, None), ring, c2)
    coarse_conv(ci_of, co_ref, list(range(2, half - 2)), coarse_ref, ring)
    lift(co_ref, up_ref, range(2, half - 2), h1_of, h2_of, lambda r: (mask, None), range(4, rows - 4), ring)
    second_conv(h2_of, h3_of, list(range(3, half - 3)), w_ref.at[1], own, c1)


def outer_kernel(
    now_ref, next_ref, odd_ref, even_ref, xin_ref, w_ref, h1in_ref, ciin_ref, h2in_ref, h3in_ref,
    coarse_ref, down_ref, up_ref, outp_ref, noisy_ref, noise_ref, out_ref,
    x_ref, pool_ref, h1_ref, ci_ref, co_ref, h2_ref, h3_ref, flat_ref, *, sizes, pieces,
):
    rows, _, ring, c1 = xin_ref.shape
    own = ring - PER
    c2 = down_ref.shape[1]
    half = rows // 2
    place = Place(sizes, pieces)
    inside = place.column_mask(ring, own)

    def mask_to(extent):
        return lambda r: (inside, place.above if r < 0 else place.below if r >= extent else None)

    low = lax.rem(place.patch, 2) == 0
    for n in range(HALO):
        above, below = [], []
        for q in range(2):
            by_odd, by_even = odd_ref[n, q].astype(F32), even_ref[n, q].astype(F32)
            above.append(jnp.where(low, by_odd, by_even))
            below.append(jnp.where(low, by_even, by_odd))
        put_planes(x_ref, n, *above)
        put_planes(x_ref, HALO + n, *below)

    def x_of(r):
        return (x_ref, r + HALO) if r < 0 else (xin_ref, r) if r < rows else (x_ref, HALO + r - rows)

    def h1_of(r):
        if 2 <= r < rows - 2:
            return h1in_ref, r - 2
        if -1 <= r < 2:
            return h1_ref, r + 1
        return (h1_ref, 3 + r - (rows - 2)) if rows - 2 <= r <= rows else None

    def ci_of(i):
        if 1 <= i < half - 1:
            return ciin_ref, i - 1
        return (ci_ref, i + 2) if i < 1 else (ci_ref, 3 + i - (half - 1))

    def h2_of(r):
        if 4 <= r < rows - 4:
            return h2in_ref, r - 4
        return (h2_ref, r + 1) if r < 4 else (h2_ref, 5 + r - (rows - 4))

    def h3_of(r):
        return (h3in_ref, r - 6) if 6 <= r < rows - 6 else (h3_ref, r) if r < 6 else (h3_ref, 6 + r - (rows - 6))

    pairs = [-2, -1, 0, half - 1, half, half + 1]
    first_conv(x_of, h1_of, pool_ref, pairs.index, pairs, w_ref.at[0], ring, c1)
    coarse_in(pool_ref, down_ref, ci_of, pairs, mask_to(half), ring, c2)
    order = [-1, 0, 1, half - 2, half - 1, half]
    coarse_conv(ci_of, co_ref, order, coarse_ref, ring)
    wanted = [r for r in range(-1, rows + 1) if not 4 <= r < rows - 4]
    lift(co_ref, up_ref, order, h1_of, h2_of, mask_to(rows), wanted, ring)
    second_conv(h2_of, h3_of, [i for i in range(half) if not 3 <= i < half - 3], w_ref.at[1], own, c1)

    spread = jnp.transpose(jnp.broadcast_to(outp_ref[...].astype(F32), (128, c1)))
    lane = lax.broadcasted_iota(jnp.int32, (c1, 128), 1)
    pick = jnp.concatenate([jnp.where(lane == r, spread, 0.0).astype(BF16) for r in range(rows)], axis=0)
    parts = []
    for q in range(2):
        found = [h3_of(r) for r in range(rows)]
        parts.append(jnp.concatenate([ref[q, at] for ref, at in found], axis=1))
    sums = jnp.dot(jnp.concatenate(parts, axis=0), pick, preferred_element_type=F32)
    for q in range(2):
        flat_ref[pl.ds(q, own, stride=2), :] = sums[q * own : (q + 1) * own]
    network = jnp.transpose(flat_ref[...])[:rows]

    level = now_ref[...]
    after = next_ref[...]
    scale_in = 1.0 / jnp.sqrt(level * level + 1.0)
    scale_skip = 1.0 / (level * level + 1.0)
    scale_out = level * scale_in
    ratio = after / level
    spread_by = jnp.sqrt(level * level - after * after)
    here = pl.ds(pl.multiple_of(place.piece * 2 * own, 128), 2 * own)
    noisy = noisy_ref[:, here]
    denoised = scale_skip * noisy + scale_out * network
    out_ref[...] = denoised + ratio * (noisy - denoised) + spread_by * noise_ref[:, here]


def near(*arrays):
    return [pltpu.with_memory_space_constraint(a, pltpu.VMEM) for a in arrays]


def per_device(
    sizes,
    noisy_field, noise_draw, cond_features, sigma_now, sigma_next, field_proj,
    fine_kernels, coarse_kernel, down_proj, up_proj, out_proj,
):
    rows, cols, c1 = cond_features.shape
    c2 = down_proj.shape[1]
    patches, copies = sizes["patch"], sizes["fsdp"]
    pieces = 2 if copies % 2 == 0 and cols % 256 == 0 else 1
    if sizes["sub"] != 2 or rows < 16:
        raise ValueError("unsupported split")
    window = cols // pieces
    own = window // 2
    ring = own + PER
    half = rows // 2
    vmem = pl.BlockSpec(memory_space=pltpu.VMEM)
    where = dict(sizes=sizes, pieces=pieces)
    limit = lambda mib: pltpu.CompilerParams(vmem_limit_bytes=mib << 20)

    mine, tile, send = pl.pallas_call(
        functools.partial(embed_kernel, **where),
        out_shape=[
            pltpu.VMEM((rows, 2, own, c1), BF16),
            pltpu.VMEM((rows, 2, PER, c1), BF16),
            pltpu.VMEM((rows, 2, PER, c1), BF16),
        ],
        in_specs=[vmem] + [pl.BlockSpec(memory_space=pltpu.HBM)] * 3,
        out_specs=[vmem] * 3,
        scratch_shapes=[
            pltpu.VMEM((rows, window, c1), BF16),
            pltpu.VMEM((rows, EDGE, c1), BF16),
            pltpu.VMEM((rows, EDGE, c1), BF16),
            pltpu.VMEM((rows, cols), F32),
            pltpu.VMEM((1, c1), F32),
            pltpu.VMEM((cols, 128), F32),
            pltpu.VMEM((2, window, c1), F32),
            pltpu.VMEM((2, 2 * EDGE, c1), F32),
            pltpu.SemaphoreType.DMA((5,)),
        ],
        compiler_params=limit(8),
        name="embed",
    )(sigma_now[None], *[pltpu.with_memory_space_constraint(a, pltpu.HBM) for a in (cond_features, noisy_field, field_proj[None])])

    got = lax.ppermute(send, "sub", [(0, 1), (1, 0)])

    packed = pl.pallas_call(
        pack_kernel,
        out_shape=pltpu.VMEM((2, 12 * c1, 2 * c1), BF16),
        in_specs=[vmem],
        out_specs=vmem,
        cost_estimate=pl.CostEstimate(flops=0, bytes_accessed=2 << 20, transcendentals=0),
        compiler_params=limit(4),
        name="pack",
    )(*near(fine_kernels))

    full, for_even, for_odd = pl.pallas_call(
        functools.partial(border_kernel, **where),
        out_shape=[
            pltpu.VMEM((rows, 2, PER, c1), BF16),
            pltpu.VMEM((HALO, 2, ring, c1), BF16),
            pltpu.VMEM((HALO, 2, ring, c1), BF16),
        ],
        in_specs=[vmem] * 3,
        out_specs=[vmem] * 3,
        compiler_params=limit(4),
        name="border",
    )(*near(mine, tile, got))

    def swap(rows_to_give, low):
        return lax.ppermute(rows_to_give, "patch", [pair for i in range(low, patches - 1, 2) for pair in ((i, i + 1), (i + 1, i))])

    odd = swap(for_odd, 1)
    even = swap(for_even, 0)

    weights = near(coarse_kernel.reshape(9 * c2, c2), down_proj, up_proj)
    work = 2 * ring * c1 * c1 * 18 * 2 * (half - 2) + 2 * ring * 9 * c2 * c2 * (half - 4)
    inner = pl.pallas_call(
        functools.partial(inner_kernel, **where),
        out_shape=[
            pltpu.VMEM((rows, 4, ring, c1), BF16),
            pltpu.VMEM((rows - 4, 2, ring, c1), BF16),
            pltpu.VMEM((half - 2, 3, ring, c2), BF16),
            pltpu.VMEM((rows - 8, 4, ring, c1), BF16),
            pltpu.VMEM((2, rows - 12, own, c1), BF16),
        ],
        in_specs=[vmem] * 6,
        out_specs=[vmem] * 5,
        scratch_shapes=[
            pltpu.VMEM(((half - 2) * ring, c1), BF16),
            pltpu.VMEM(((half - 4) * ring, c2), BF16),
        ],
        cost_estimate=pl.CostEstimate(flops=work * 2, bytes_accessed=4 << 20, transcendentals=0),
        compiler_params=limit(12),
        name="inner",
    )(*near(mine, full, packed), *weights)

    part = pl.pallas_call(
        functools.partial(outer_kernel, **where),
        out_shape=pltpu.VMEM((rows, window), F32),
        in_specs=[vmem] * 16,
        out_specs=vmem,
        scratch_shapes=[
            pltpu.VMEM((2 * HALO, 4, ring, c1), BF16),
            pltpu.VMEM((6 * ring, c1), BF16),
            pltpu.VMEM((6, 2, ring, c1), BF16),
            pltpu.VMEM((6, 3, ring, c2), BF16),
            pltpu.VMEM((6 * ring, c2), BF16),
            pltpu.VMEM((10, 4, ring, c1), BF16),
            pltpu.VMEM((2, 12, own, c1), BF16),
            pltpu.VMEM((window, 128), F32),
        ],
        compiler_params=limit(16),
        name="outer",
    )(sigma_now[None], sigma_next[None], *near(odd, even, *inner[:1], packed, *inner[1:]), *weights, *near(out_proj[None], noisy_field, noise_draw))
    if pieces == 1:
        return part
    other = lax.ppermute(part, "fsdp", [(i, i ^ 1) for i in range(copies)])
    first = lax.rem(lax.axis_index("fsdp"), pieces) == 0
    return jnp.where(first, jnp.concatenate([part, other], axis=1), jnp.concatenate([other, part], axis=1))


def solution(mesh):
    return jax.shard_map(
        functools.partial(per_device, dict(mesh.shape)),
        mesh=mesh,
        in_specs=(
            P(("groups", "patch"), "sub"),
            P(("groups", "patch"), "sub"),
            P(("groups", "patch"), "sub", None),
            P(),
            P(),
            P(),
            P(),
            P(),
            P(),
            P(),
            P(),
        ),
        out_specs=P(("groups", "patch"), "sub"),
        check_vma=False,
    )
```

```python
import functools

import jax
import jax.numpy as jnp
from jax import lax
from jax.experimental import pallas as pl
from jax.experimental.pallas import tpu as pltpu
from jax.sharding import PartitionSpec as P

F32 = jnp.float32
BF16 = jnp.bfloat16
HALO = 5
EDGE = 16
PER = EDGE // 2
CHUNK = 3


def silu_of_half(half):
    return half + half * jnp.tanh(half)


def silu(v):
    return silu_of_half(0.5 * v)


def flag(condition):
    return jnp.where(condition, 1.0, 0.0).astype(F32)


class Place:
    def __init__(self, sizes, pieces):
        self.piece = lax.rem(lax.axis_index("fsdp"), pieces)
        self.sub = lax.axis_index("sub")
        self.patch = lax.axis_index("patch")
        self.first = self.piece == 0
        self.last = self.piece == pieces - 1
        self.has_left = jnp.logical_or(self.piece > 0, self.sub > 0)
        self.has_right = jnp.logical_or(self.piece < pieces - 1, self.sub < sizes["sub"] - 1)
        self.above = flag(self.patch > 0)
        self.below = flag(self.patch < sizes["patch"] - 1)

    def column_mask(self, ring, own):
        at = lax.broadcasted_iota(jnp.int32, (ring, 128), 0)
        return jnp.where(at < own, 1.0, jnp.where(at < own + PER // 2, flag(self.has_right), flag(self.has_left)))


def embed_kernel(
    now_ref, cond_ref, noisy_ref, proj_ref, mine_ref, tile_ref, send_ref,
    main, inner, give, field, embedding, turned, wide, edge, sems, *, sizes, pieces,
):
    rows, window, _ = main.shape
    cols = noisy_ref.shape[1]
    place = Place(sizes, pieces)
    start = pl.multiple_of(place.piece * window, EDGE)
    near_by = pl.multiple_of(jnp.where(place.first, window, start - EDGE), EDGE)
    given = pl.multiple_of(jnp.where(place.sub == 0, cols - EDGE, 0), EDGE)
    small = [
        pltpu.make_async_copy(noisy_ref, field, sems.at[3]),
        pltpu.make_async_copy(proj_ref, embedding, sems.at[4]),
    ]
    copies = [pltpu.make_async_copy(cond_ref.at[:, pl.ds(given, EDGE)], give, sems.at[0])]
    if pieces > 1:
        copies.append(pltpu.make_async_copy(cond_ref.at[:, pl.ds(near_by, EDGE)], inner, sems.at[1]))
    copies.append(pltpu.make_async_copy(cond_ref.at[:, pl.ds(start, window)], main, sems.at[2]))
    for copy in small + copies:
        copy.start()
    for copy in small:
        copy.wait()
    level = now_ref[...]
    scale_in = 1.0 / jnp.sqrt(level * level + 1.0)
    scaled = field[...] * scale_in
    high = scaled.astype(BF16).astype(F32)
    middle = (scaled - high).astype(BF16).astype(F32)
    low = scaled - high - middle
    fill = jnp.zeros((128 - 3 * rows, cols), F32)
    turned[...] = jnp.transpose(jnp.concatenate([high, middle, low, fill], axis=0)).astype(BF16)
    proj = embedding[...]
    c1 = proj.shape[1]
    head = lax.broadcasted_iota(jnp.int32, (PER, 128), 0) < PER // 2

    lhs = jnp.concatenate([turned[pl.ds(at, n)] for at, n in ((start, window), (given, EDGE), (near_by, EDGE))], axis=0)
    term = lax.broadcasted_iota(jnp.int32, (128, 2 * c1), 0)
    right_half = jnp.where(lax.broadcasted_iota(jnp.int32, (128, 2 * c1), 1) < c1, 0, 1)
    for r in range(0, rows, 2):
        wanted = right_half + r
        pick = jnp.where(term == wanted, 1.0, 0.0)
        for k in (1, 2):
            pick = jnp.where(term == wanted + k * rows, 1.0, pick)
        spread = jnp.dot(lhs, pick.astype(BF16), preferred_element_type=F32)
        for o in range(2):
            product = spread[:, o * c1 : (o + 1) * c1] * proj
            wide[r + o] = product[:window]
            edge[r + o] = product[window:]
    for copy in copies[:-1]:
        copy.wait()
    for r in range(rows):
        edge[r, :EDGE] = give[r].astype(F32) + edge[r, :EDGE]
        for q in range(2):
            send_ref[r, q] = edge[r, pl.ds(q, PER, stride=2), :].astype(BF16)
        if pieces > 1:
            edge[r, EDGE:] = inner[r].astype(F32) + edge[r, EDGE:]
            for q in range(2):
                block = edge[r, pl.ds(EDGE + q, PER, stride=2), :]
                to_right = block * flag(jnp.logical_not(place.last))
                to_left = block * flag(jnp.logical_not(place.first))
                tile_ref[r, q] = jnp.where(head, to_right, to_left).astype(BF16)
        else:
            tile_ref[r] = jnp.zeros_like(tile_ref[r])
    copies[-1].wait()
    for r in range(rows):
        wide[r] = main[r].astype(F32) + wide[r]
        for q in range(2):
            mine_ref[r, q] = wide[r, pl.ds(q, window // 2, stride=2), :].astype(BF16)


def border_kernel(mine_ref, tile_ref, got_ref, full_ref, even_ref, odd_ref, *, sizes, pieces):
    rows, _, own, _ = mine_ref.shape
    place = Place(sizes, pieces)
    right = flag(jnp.logical_and(place.last, place.has_right))
    left = flag(jnp.logical_and(place.first, place.has_left))
    head = lax.broadcasted_iota(jnp.int32, (PER, 128), 0) < PER // 2
    for r in range(rows):
        for q in range(2):
            got = got_ref[r, q].astype(F32)
            tile = tile_ref[r, q].astype(F32) + jnp.where(head, got * right, got * left)
            full_ref[r, q] = tile.astype(BF16)
    low = lax.rem(place.patch, 2) == 0
    for ref, start in ((even_ref, jnp.where(low, rows - HALO, 0)), (odd_ref, jnp.where(low, 0, rows - HALO))):
        for n in range(HALO):
            ref[n, :, :own] = mine_ref[start + n]
            ref[n, :, own:] = full_ref[start + n]


def put_planes(ref, at, even, odd):
    ring = even.shape[0]
    ref[at, 0] = even.astype(BF16)
    ref[at, 1] = odd.astype(BF16)
    ref[at, 2] = pltpu.roll(odd, 1, 0).astype(BF16)
    ref[at, 3] = pltpu.roll(even, ring - 1, 0).astype(BF16)


def masked(x, columns, row):
    own = x.shape[0] - PER
    columns = jnp.concatenate([columns[own:]] * (x.shape[1] // 128), axis=1)
    x = jnp.concatenate([x[:own], x[own:] * columns], axis=0)
    return x if row is None else x * row


def chunks(rows_of):
    return [rows_of[k : k + CHUNK] for k in range(0, len(rows_of), CHUNK)]


def conv_pairs(planes_of, pairs, weight, kept):
    parts = []
    for i in pairs:
        found = [planes_of(2 * i - 1 + d) for d in range(4)]
        for planes in ((2, 0, 1), (0, 1, 3)):
            parts.append(jnp.concatenate([ref[at, k, :kept] for k in planes for ref, at in found], axis=1))
    return jnp.dot(jnp.concatenate(parts, axis=0), weight[...], preferred_element_type=F32)


def first_conv(planes_of, h1_of, pool_ref, slot_of, pairs, weight, ring, c1):
    for group in chunks(pairs):
        acc = conv_pairs(planes_of, group, weight, ring)
        for n, i in enumerate(group):
            total = None
            for o in range(2):
                ref, at = planes_of(2 * i + o)
                for q in range(2):
                    v = acc[(2 * n + q) * ring : (2 * n + q + 1) * ring, o * c1 : (o + 1) * c1]
                    h = (ref[at, q].astype(F32) + silu_of_half(v)).astype(BF16)
                    kept = h1_of(2 * i + o)
                    if kept is not None:
                        kept[0][kept[1], q] = h
                    total = h.astype(F32) if total is None else total + h.astype(F32)
            pool_ref[slot_of(i) * ring : (slot_of(i) + 1) * ring] = (total * 0.25).astype(BF16)


def coarse_in(pool_ref, down_ref, ci_of, order, mask_of, ring, c2):
    ci_all = jnp.dot(pool_ref[...], down_ref[...], preferred_element_type=F32)
    for n, i in enumerate(order):
        ci = masked(ci_all[n * ring : (n + 1) * ring], *mask_of(i))
        ref, at = ci_of(i)
        ref[at, 0] = pltpu.roll(ci, 1, 0).astype(BF16)
        ref[at, 1] = ci.astype(BF16)
        ref[at, 2] = pltpu.roll(ci, ring - 1, 0).astype(BF16)


def coarse_conv(ci_of, co_ref, order, coarse_ref, ring):
    for k, group in enumerate(chunks(order)):
        parts = []
        for i in group:
            found = [ci_of(i - 1 + a) for a in range(3)]
            parts.append(jnp.concatenate([ref[at, b] for ref, at in found for b in range(3)], axis=1))
        v = jnp.dot(jnp.concatenate(parts, axis=0), coarse_ref[...], preferred_element_type=F32)
        for n, i in enumerate(group):
            ref, at = ci_of(i)
            slot = k * CHUNK + n
            co = ref[at, 1].astype(F32) + silu(v[n * ring : (n + 1) * ring])
            co_ref[slot * ring : (slot + 1) * ring] = co.astype(BF16)


def lift(co_ref, up_ref, order, h1_of, h2_of, mask_of, wanted, ring):
    lifted_all = jnp.dot(co_ref[...], up_ref[...], preferred_element_type=F32)
    for n, i in enumerate(order):
        lifted = lifted_all[n * ring : (n + 1) * ring]
        for r in (2 * i, 2 * i + 1):
            if r in wanted:
                ref, at = h1_of(r)
                mask = mask_of(r)
                into, slot = h2_of(r)
                put_planes(into, slot, *(masked(ref[at, q].astype(F32) + lifted, *mask) for q in range(2)))


def second_conv(h2_of, h3_of, pairs, weight, own, c1):
    for group in chunks(pairs):
        acc = conv_pairs(h2_of, group, weight, own)
        for n, i in enumerate(group):
            for o in range(2):
                ref, at = h2_of(2 * i + o)
                into, slot = h3_of(2 * i + o)
                for q in range(2):
                    v = acc[(2 * n + q) * own : (2 * n + q + 1) * own, o * c1 : (o + 1) * c1]
                    into[q, slot] = (ref[at, q, :own].astype(F32) + silu_of_half(v)).astype(BF16)


def pack_kernel(fine_ref, w_ref):
    c1 = fine_ref.shape[3]
    for layer in range(2):
        for b in range(3):
            for d in range(4):
                at = (b * 4 + d) * c1
                for o in range(2):
                    a = d - o
                    block = fine_ref[layer, a * 3 + b] * 0.5 if 0 <= a <= 2 else jnp.zeros((c1, c1), BF16)
                    w_ref[layer, at : at + c1, o * c1 : (o + 1) * c1] = block


def inner_kernel(
    mine_ref, tile_ref, w_ref, coarse_ref, down_ref, up_ref,
    x_ref, h1_ref, ci_ref, h2_ref, h3_ref, pool_ref, co_ref, *, sizes, pieces,
):
    rows, _, own, c1 = mine_ref.shape
    ring = own + PER
    c2 = down_ref.shape[1]
    half = rows // 2
    mask = Place(sizes, pieces).column_mask(ring, own)
    for r in range(rows):
        even, odd = (jnp.concatenate([mine_ref[r, q].astype(F32), tile_ref[r, q].astype(F32)], axis=0) for q in range(2))
        put_planes(x_ref, r, even, odd)
    x_of = lambda r: (x_ref, r)
    h1_of = lambda r: (h1_ref, r - 2)
    ci_of = lambda i: (ci_ref, i - 1)
    h2_of = lambda r: (h2_ref, r - 4)
    h3_of = lambda r: (h3_ref, r - 6)
    first_conv(x_of, h1_of, pool_ref, lambda i: i - 1, list(range(1, half - 1)), w_ref.at[0], ring, c1)
    coarse_in(pool_ref, down_ref, ci_of, range(1, half - 1), lambda i: (mask, None), ring, c2)
    coarse_conv(ci_of, co_ref, list(range(2, half - 2)), coarse_ref, ring)
    lift(co_ref, up_ref, range(2, half - 2), h1_of, h2_of, lambda r: (mask, None), range(4, rows - 4), ring)
    second_conv(h2_of, h3_of, list(range(3, half - 3)), w_ref.at[1], own, c1)


def outer_kernel(
    now_ref, next_ref, odd_ref, even_ref, xin_ref, w_ref, h1in_ref, ciin_ref, h2in_ref, h3in_ref,
    coarse_ref, down_ref, up_ref, outp_ref, noisy_ref, noise_ref, out_ref,
    x_ref, pool_ref, h1_ref, ci_ref, co_ref, h2_ref, h3_ref, flat_ref, *, sizes, pieces,
):
    rows, _, ring, c1 = xin_ref.shape
    own = ring - PER
    c2 = down_ref.shape[1]
    half = rows // 2
    place = Place(sizes, pieces)
    inside = place.column_mask(ring, own)

    def mask_to(extent):
        return lambda r: (inside, place.above if r < 0 else place.below if r >= extent else None)

    low = lax.rem(place.patch, 2) == 0
    for n in range(HALO):
        above, below = [], []
        for q in range(2):
            by_odd, by_even = odd_ref[n, q].astype(F32), even_ref[n, q].astype(F32)
            above.append(jnp.where(low, by_odd, by_even))
            below.append(jnp.where(low, by_even, by_odd))
        put_planes(x_ref, n, *above)
        put_planes(x_ref, HALO + n, *below)

    def x_of(r):
        return (x_ref, r + HALO) if r < 0 else (xin_ref, r) if r < rows else (x_ref, HALO + r - rows)

    def h1_of(r):
        if 2 <= r < rows - 2:
            return h1in_ref, r - 2
        if -1 <= r < 2:
            return h1_ref, r + 1
        return (h1_ref, 3 + r - (rows - 2)) if rows - 2 <= r <= rows else None

    def ci_of(i):
        if 1 <= i < half - 1:
            return ciin_ref, i - 1
        return (ci_ref, i + 2) if i < 1 else (ci_ref, 3 + i - (half - 1))

    def h2_of(r):
        if 4 <= r < rows - 4:
            return h2in_ref, r - 4
        return (h2_ref, r + 1) if r < 4 else (h2_ref, 5 + r - (rows - 4))

    def h3_of(r):
        return (h3in_ref, r - 6) if 6 <= r < rows - 6 else (h3_ref, r) if r < 6 else (h3_ref, 6 + r - (rows - 6))

    pairs = [-2, -1, 0, half - 1, half, half + 1]
    first_conv(x_of, h1_of, pool_ref, pairs.index, pairs, w_ref.at[0], ring, c1)
    coarse_in(pool_ref, down_ref, ci_of, pairs, mask_to(half), ring, c2)
    order = [-1, 0, 1, half - 2, half - 1, half]
    coarse_conv(ci_of, co_ref, order, coarse_ref, ring)
    wanted = [r for r in range(-1, rows + 1) if not 4 <= r < rows - 4]
    lift(co_ref, up_ref, order, h1_of, h2_of, mask_to(rows), wanted, ring)
    second_conv(h2_of, h3_of, [i for i in range(half) if not 3 <= i < half - 3], w_ref.at[1], own, c1)

    spread = jnp.transpose(jnp.broadcast_to(outp_ref[...].astype(F32), (128, c1)))
    lane = lax.broadcasted_iota(jnp.int32, (c1, 128), 1)
    pick = jnp.concatenate([jnp.where(lane == r, spread, 0.0).astype(BF16) for r in range(rows)], axis=0)
    parts = []
    for q in range(2):
        found = [h3_of(r) for r in range(rows)]
        parts.append(jnp.concatenate([ref[q, at] for ref, at in found], axis=1))
    sums = jnp.dot(jnp.concatenate(parts, axis=0), pick, preferred_element_type=F32)
    for q in range(2):
        flat_ref[pl.ds(q, own, stride=2), :] = sums[q * own : (q + 1) * own]
    network = jnp.transpose(flat_ref[...])[:rows]

    level = now_ref[...]
    after = next_ref[...]
    scale_in = 1.0 / jnp.sqrt(level * level + 1.0)
    scale_skip = 1.0 / (level * level + 1.0)
    scale_out = level * scale_in
    ratio = after / level
    spread_by = jnp.sqrt(level * level - after * after)
    here = pl.ds(pl.multiple_of(place.piece * 2 * own, 128), 2 * own)
    noisy = noisy_ref[:, here]
    denoised = scale_skip * noisy + scale_out * network
    out_ref[...] = denoised + ratio * (noisy - denoised) + spread_by * noise_ref[:, here]


def near(*arrays):
    return [pltpu.with_memory_space_constraint(a, pltpu.VMEM) for a in arrays]


def per_device(
    sizes,
    noisy_field, noise_draw, cond_features, sigma_now, sigma_next, field_proj,
    fine_kernels, coarse_kernel, down_proj, up_proj, out_proj,
):
    rows, cols, c1 = cond_features.shape
    c2 = down_proj.shape[1]
    patches, copies = sizes["patch"], sizes["fsdp"]
    pieces = 2 if copies % 2 == 0 and cols % 256 == 0 else 1
    if sizes["sub"] != 2 or rows < 16 or rows > 42 or rows % 2:
        raise ValueError("unsupported split")
    window = cols // pieces
    own = window // 2
    ring = own + PER
    half = rows // 2
    vmem = pl.BlockSpec(memory_space=pltpu.VMEM)
    where = dict(sizes=sizes, pieces=pieces)
    limit = lambda mib: pltpu.CompilerParams(vmem_limit_bytes=mib << 20)

    mine, tile, send = pl.pallas_call(
        functools.partial(embed_kernel, **where),
        out_shape=[
            pltpu.VMEM((rows, 2, own, c1), BF16),
            pltpu.VMEM((rows, 2, PER, c1), BF16),
            pltpu.VMEM((rows, 2, PER, c1), BF16),
        ],
        in_specs=[vmem] + [pl.BlockSpec(memory_space=pltpu.HBM)] * 3,
        out_specs=[vmem] * 3,
        scratch_shapes=[
            pltpu.VMEM((rows, window, c1), BF16),
            pltpu.VMEM((rows, EDGE, c1), BF16),
            pltpu.VMEM((rows, EDGE, c1), BF16),
            pltpu.VMEM((rows, cols), F32),
            pltpu.VMEM((1, c1), F32),
            pltpu.VMEM((cols, 128), BF16),
            pltpu.VMEM((rows, window, c1), F32),
            pltpu.VMEM((rows, 2 * EDGE, c1), F32),
            pltpu.SemaphoreType.DMA((5,)),
        ],
        compiler_params=limit(8),
        name="embed",
    )(sigma_now[None], *[pltpu.with_memory_space_constraint(a, pltpu.HBM) for a in (cond_features, noisy_field, field_proj[None])])

    got = lax.ppermute(send, "sub", [(0, 1), (1, 0)])

    packed = pl.pallas_call(
        pack_kernel,
        out_shape=pltpu.VMEM((2, 12 * c1, 2 * c1), BF16),
        in_specs=[vmem],
        out_specs=vmem,
        cost_estimate=pl.CostEstimate(flops=0, bytes_accessed=2 << 20, transcendentals=0),
        compiler_params=limit(4),
        name="pack",
    )(*near(fine_kernels))

    full, for_even, for_odd = pl.pallas_call(
        functools.partial(border_kernel, **where),
        out_shape=[
            pltpu.VMEM((rows, 2, PER, c1), BF16),
            pltpu.VMEM((HALO, 2, ring, c1), BF16),
            pltpu.VMEM((HALO, 2, ring, c1), BF16),
        ],
        in_specs=[vmem] * 3,
        out_specs=[vmem] * 3,
        compiler_params=limit(4),
        name="border",
    )(*near(mine, tile, got))

    def swap(rows_to_give, low):
        return lax.ppermute(rows_to_give, "patch", [pair for i in range(low, patches - 1, 2) for pair in ((i, i + 1), (i + 1, i))])

    odd = swap(for_odd, 1)
    even = swap(for_even, 0)

    weights = near(coarse_kernel.reshape(9 * c2, c2), down_proj, up_proj)
    work = 2 * ring * c1 * c1 * 18 * 2 * (half - 2) + 2 * ring * 9 * c2 * c2 * (half - 4)
    inner = pl.pallas_call(
        functools.partial(inner_kernel, **where),
        out_shape=[
            pltpu.VMEM((rows, 4, ring, c1), BF16),
            pltpu.VMEM((rows - 4, 2, ring, c1), BF16),
            pltpu.VMEM((half - 2, 3, ring, c2), BF16),
            pltpu.VMEM((rows - 8, 4, ring, c1), BF16),
            pltpu.VMEM((2, rows - 12, own, c1), BF16),
        ],
        in_specs=[vmem] * 6,
        out_specs=[vmem] * 5,
        scratch_shapes=[
            pltpu.VMEM(((half - 2) * ring, c1), BF16),
            pltpu.VMEM(((half - 4) * ring, c2), BF16),
        ],
        cost_estimate=pl.CostEstimate(flops=work * 2, bytes_accessed=4 << 20, transcendentals=0),
        compiler_params=limit(12),
        name="inner",
    )(*near(mine, full, packed), *weights)

    part = pl.pallas_call(
        functools.partial(outer_kernel, **where),
        out_shape=pltpu.VMEM((rows, window), F32),
        in_specs=[vmem] * 16,
        out_specs=vmem,
        scratch_shapes=[
            pltpu.VMEM((2 * HALO, 4, ring, c1), BF16),
            pltpu.VMEM((6 * ring, c1), BF16),
            pltpu.VMEM((6, 2, ring, c1), BF16),
            pltpu.VMEM((6, 3, ring, c2), BF16),
            pltpu.VMEM((6 * ring, c2), BF16),
            pltpu.VMEM((10, 4, ring, c1), BF16),
            pltpu.VMEM((2, 12, own, c1), BF16),
            pltpu.VMEM((window, 128), F32),
        ],
        compiler_params=limit(16),
        name="outer",
    )(sigma_now[None], sigma_next[None], *near(odd, even, *inner[:1], packed, *inner[1:]), *weights, *near(out_proj[None], noisy_field, noise_draw))
    if pieces == 1:
        return part
    other = lax.ppermute(part, "fsdp", [(i, i ^ 1) for i in range(copies)])
    first = lax.rem(lax.axis_index("fsdp"), pieces) == 0
    return jnp.where(first, jnp.concatenate([part, other], axis=1), jnp.concatenate([other, part], axis=1))


def solution(mesh):
    return jax.shard_map(
        functools.partial(per_device, dict(mesh.shape)),
        mesh=mesh,
        in_specs=(
            P(("groups", "patch"), "sub"),
            P(("groups", "patch"), "sub"),
            P(("groups", "patch"), "sub", None),
            P(),
            P(),
            P(),
            P(),
            P(),
            P(),
            P(),
            P(),
        ),
        out_specs=P(("groups", "patch"), "sub"),
        check_vma=False,
    )
```

```python
import functools

import jax
import jax.numpy as jnp
from jax import lax
from jax.experimental import pallas as pl
from jax.experimental.pallas import tpu as pltpu
from jax.sharding import PartitionSpec as P

F32 = jnp.float32
BF16 = jnp.bfloat16
HALO = 5
EDGE = 16
PER = EDGE // 2
CHUNK = 3


def silu_of_half(half):
    return half + half * jnp.tanh(half)


def silu(v):
    return silu_of_half(0.5 * v)


def flag(condition):
    return jnp.where(condition, 1.0, 0.0).astype(F32)


class Place:
    def __init__(self, sizes, pieces):
        self.piece = lax.rem(lax.axis_index("fsdp"), pieces)
        self.sub = lax.axis_index("sub")
        self.patch = lax.axis_index("patch")
        self.first = self.piece == 0
        self.last = self.piece == pieces - 1
        self.has_left = jnp.logical_or(self.piece > 0, self.sub > 0)
        self.has_right = jnp.logical_or(self.piece < pieces - 1, self.sub < sizes["sub"] - 1)
        self.above = flag(self.patch > 0)
        self.below = flag(self.patch < sizes["patch"] - 1)

    def column_mask(self, ring, own):
        at = lax.broadcasted_iota(jnp.int32, (ring, 128), 0)
        return jnp.where(at < own, 1.0, jnp.where(at < own + PER // 2, flag(self.has_right), flag(self.has_left)))


def embed_kernel(
    now_ref, cond_ref, noisy_ref, proj_ref, mine_ref, tile_ref, send_ref,
    main, inner, give, field, embedding, turned, wide, edge, sems, *, sizes, pieces,
):
    rows, window, _ = main.shape
    cols = noisy_ref.shape[1]
    place = Place(sizes, pieces)
    start = pl.multiple_of(place.piece * window, EDGE)
    near_by = pl.multiple_of(jnp.where(place.first, window, start - EDGE), EDGE)
    given = pl.multiple_of(jnp.where(place.sub == 0, cols - EDGE, 0), EDGE)
    small = [
        pltpu.make_async_copy(noisy_ref, field, sems.at[3]),
        pltpu.make_async_copy(proj_ref, embedding, sems.at[4]),
    ]
    copies = [pltpu.make_async_copy(cond_ref.at[:, pl.ds(given, EDGE)], give, sems.at[0])]
    if pieces > 1:
        copies.append(pltpu.make_async_copy(cond_ref.at[:, pl.ds(near_by, EDGE)], inner, sems.at[1]))
    copies.append(pltpu.make_async_copy(cond_ref.at[:, pl.ds(start, window)], main, sems.at[2]))
    for copy in small + copies:
        copy.start()
    for copy in small:
        copy.wait()
    level = now_ref[...]
    scale_in = 1.0 / jnp.sqrt(level * level + 1.0)
    scaled = field[...] * scale_in
    high = scaled.astype(BF16).astype(F32)
    middle = (scaled - high).astype(BF16).astype(F32)
    low = scaled - high - middle
    fill = jnp.zeros((128 - 3 * rows, cols), F32)
    turned[...] = jnp.transpose(jnp.concatenate([high, middle, low, fill], axis=0)).astype(BF16)
    proj = embedding[...]
    c1 = proj.shape[1]
    head = lax.broadcasted_iota(jnp.int32, (PER, 128), 0) < PER // 2

    lhs = jnp.concatenate([turned[pl.ds(at, n)] for at, n in ((start, window), (given, EDGE), (near_by, EDGE))], axis=0)
    term = lax.broadcasted_iota(jnp.int32, (128, 2 * c1), 0)
    right_half = jnp.where(lax.broadcasted_iota(jnp.int32, (128, 2 * c1), 1) < c1, 0, 1)
    for r in range(0, rows, 2):
        wanted = right_half + r
        pick = jnp.where(term == wanted, 1.0, 0.0)
        for k in (1, 2):
            pick = jnp.where(term == wanted + k * rows, 1.0, pick)
        spread = jnp.dot(lhs, pick.astype(BF16), preferred_element_type=F32)
        for o in range(2):
            product = spread[:, o * c1 : (o + 1) * c1] * proj
            wide[r + o] = product[:window]
            edge[r + o] = product[window:]
    for copy in copies[:-1]:
        copy.wait()
    for r in range(rows):
        edge[r, :EDGE] = give[r].astype(F32) + edge[r, :EDGE]
        for q in range(2):
            send_ref[r, q] = edge[r, pl.ds(q, PER, stride=2), :].astype(BF16)
        if pieces > 1:
            edge[r, EDGE:] = inner[r].astype(F32) + edge[r, EDGE:]
            for q in range(2):
                block = edge[r, pl.ds(EDGE + q, PER, stride=2), :]
                to_right = block * flag(jnp.logical_not(place.last))
                to_left = block * flag(jnp.logical_not(place.first))
                tile_ref[r, q] = jnp.where(head, to_right, to_left).astype(BF16)
        else:
            tile_ref[r] = jnp.zeros_like(tile_ref[r])
    copies[-1].wait()
    for r in range(rows):
        wide[r] = main[r].astype(F32) + wide[r]
        for q in range(2):
            mine_ref[r, q] = wide[r, pl.ds(q, window // 2, stride=2), :].astype(BF16)


def border_kernel(mine_ref, tile_ref, got_ref, full_ref, even_ref, odd_ref, *, sizes, pieces):
    rows, _, own, _ = mine_ref.shape
    place = Place(sizes, pieces)
    right = flag(jnp.logical_and(place.last, place.has_right))
    left = flag(jnp.logical_and(place.first, place.has_left))
    head = lax.broadcasted_iota(jnp.int32, (PER, 128), 0) < PER // 2
    for r in range(rows):
        for q in range(2):
            got = got_ref[r, q].astype(F32)
            tile = tile_ref[r, q].astype(F32) + jnp.where(head, got * right, got * left)
            full_ref[r, q] = tile.astype(BF16)
    low = lax.rem(place.patch, 2) == 0
    for ref, start in ((even_ref, jnp.where(low, rows - HALO, 0)), (odd_ref, jnp.where(low, 0, rows - HALO))):
        for n in range(HALO):
            ref[n, :, :own] = mine_ref[start + n]
            ref[n, :, own:] = full_ref[start + n]


def put_planes(ref, at, even, odd):
    ring = even.shape[0]
    ref[at, 0] = even.astype(BF16)
    ref[at, 1] = odd.astype(BF16)
    ref[at, 2] = pltpu.roll(odd, 1, 0).astype(BF16)
    ref[at, 3] = pltpu.roll(even, ring - 1, 0).astype(BF16)


def masked(x, columns, row):
    own = x.shape[0] - PER
    columns = jnp.concatenate([columns[own:]] * (x.shape[1] // 128), axis=1)
    x = jnp.concatenate([x[:own], x[own:] * columns], axis=0)
    return x if row is None else x * row


def chunks(rows_of):
    return [rows_of[k : k + CHUNK] for k in range(0, len(rows_of), CHUNK)]


def conv_pairs(planes_of, pairs, weight, kept):
    parts = []
    for i in pairs:
        found = [planes_of(2 * i - 1 + d) for d in range(4)]
        for planes in ((2, 0, 1), (0, 1, 3)):
            parts.append(jnp.concatenate([ref[at, k, :kept] for k in planes for ref, at in found], axis=1))
    return jnp.dot(jnp.concatenate(parts, axis=0), weight[...], preferred_element_type=F32)


def first_conv(planes_of, h1_of, pool_ref, slot_of, pairs, weight, ring, c1):
    for group in chunks(pairs):
        acc = conv_pairs(planes_of, group, weight, ring)
        for n, i in enumerate(group):
            total = None
            for o in range(2):
                ref, at = planes_of(2 * i + o)
                for q in range(2):
                    v = acc[(2 * n + q) * ring : (2 * n + q + 1) * ring, o * c1 : (o + 1) * c1]
                    h = (ref[at, q].astype(F32) + silu_of_half(v)).astype(BF16)
                    kept = h1_of(2 * i + o)
                    if kept is not None:
                        kept[0][kept[1], q] = h
                    total = h.astype(F32) if total is None else total + h.astype(F32)
            pool_ref[slot_of(i) * ring : (slot_of(i) + 1) * ring] = (total * 0.25).astype(BF16)


def coarse_in(pool_ref, down_ref, ci_of, order, mask_of, ring, c2):
    ci_all = jnp.dot(pool_ref[...], down_ref[...], preferred_element_type=F32)
    for n, i in enumerate(order):
        ci = masked(ci_all[n * ring : (n + 1) * ring], *mask_of(i))
        ref, at = ci_of(i)
        ref[at, 0] = pltpu.roll(ci, 1, 0).astype(BF16)
        ref[at, 1] = ci.astype(BF16)
        ref[at, 2] = pltpu.roll(ci, ring - 1, 0).astype(BF16)


def coarse_conv(ci_of, co_ref, order, coarse_ref, ring):
    for k, group in enumerate(chunks(order)):
        parts = []
        for i in group:
            found = [ci_of(i - 1 + a) for a in range(3)]
            parts.append(jnp.concatenate([ref[at, b] for ref, at in found for b in range(3)], axis=1))
        v = jnp.dot(jnp.concatenate(parts, axis=0), coarse_ref[...], preferred_element_type=F32)
        for n, i in enumerate(group):
            ref, at = ci_of(i)
            slot = k * CHUNK + n
            co = ref[at, 1].astype(F32) + silu(v[n * ring : (n + 1) * ring])
            co_ref[slot * ring : (slot + 1) * ring] = co.astype(BF16)


def lift(co_ref, up_ref, order, h1_of, h2_of, mask_of, wanted, ring):
    lifted_all = jnp.dot(co_ref[...], up_ref[...], preferred_element_type=F32)
    for n, i in enumerate(order):
        lifted = lifted_all[n * ring : (n + 1) * ring]
        for r in (2 * i, 2 * i + 1):
            if r in wanted:
                ref, at = h1_of(r)
                mask = mask_of(r)
                into, slot = h2_of(r)
                put_planes(into, slot, *(masked(ref[at, q].astype(F32) + lifted, *mask) for q in range(2)))


def second_conv(h2_of, h3_of, pairs, weight, own, c1):
    for group in chunks(pairs):
        acc = conv_pairs(h2_of, group, weight, own)
        for n, i in enumerate(group):
            for o in range(2):
                ref, at = h2_of(2 * i + o)
                into, slot = h3_of(2 * i + o)
                for q in range(2):
                    v = acc[(2 * n + q) * own : (2 * n + q + 1) * own, o * c1 : (o + 1) * c1]
                    into[q, slot] = (ref[at, q, :own].astype(F32) + silu_of_half(v)).astype(BF16)


def pack_kernel(fine_ref, w_ref):
    c1 = fine_ref.shape[3]
    for layer in range(2):
        for b in range(3):
            for d in range(4):
                at = (b * 4 + d) * c1
                for o in range(2):
                    a = d - o
                    block = fine_ref[layer, a * 3 + b] * 0.5 if 0 <= a <= 2 else jnp.zeros((c1, c1), BF16)
                    w_ref[layer, at : at + c1, o * c1 : (o + 1) * c1] = block


def inner_kernel(
    mine_ref, tile_ref, w_ref, coarse_ref, down_ref, up_ref,
    x_ref, h1_ref, ci_ref, h2_ref, h3_ref, pool_ref, co_ref, *, sizes, pieces,
):
    rows, _, own, c1 = mine_ref.shape
    ring = own + PER
    c2 = down_ref.shape[1]
    half = rows // 2
    mask = Place(sizes, pieces).column_mask(ring, own)
    for r in range(rows):
        even, odd = (jnp.concatenate([mine_ref[r, q].astype(F32), tile_ref[r, q].astype(F32)], axis=0) for q in range(2))
        put_planes(x_ref, r, even, odd)
    x_of = lambda r: (x_ref, r)
    h1_of = lambda r: (h1_ref, r - 2)
    ci_of = lambda i: (ci_ref, i - 1)
    h2_of = lambda r: (h2_ref, r - 4)
    h3_of = lambda r: (h3_ref, r - 6)
    first_conv(x_of, h1_of, pool_ref, lambda i: i - 1, list(range(1, half - 1)), w_ref.at[0], ring, c1)
    coarse_in(pool_ref, down_ref, ci_of, range(1, half - 1), lambda i: (mask, None), ring, c2)
    coarse_conv(ci_of, co_ref, list(range(2, half - 2)), coarse_ref, ring)
    lift(co_ref, up_ref, range(2, half - 2), h1_of, h2_of, lambda r: (mask, None), range(4, rows - 4), ring)
    second_conv(h2_of, h3_of, list(range(3, half - 3)), w_ref.at[1], own, c1)


def outer_kernel(
    now_ref, next_ref, odd_ref, even_ref, xin_ref, w_ref, h1in_ref, ciin_ref, h2in_ref, h3in_ref,
    coarse_ref, down_ref, up_ref, outp_ref, noisy_ref, noise_ref, out_ref,
    x_ref, pool_ref, h1_ref, ci_ref, co_ref, h2_ref, h3_ref, flat_ref, *, sizes, pieces,
):
    rows, _, ring, c1 = xin_ref.shape
    own = ring - PER
    c2 = down_ref.shape[1]
    half = rows // 2
    place = Place(sizes, pieces)
    inside = place.column_mask(ring, own)

    def mask_to(extent):
        return lambda r: (inside, place.above if r < 0 else place.below if r >= extent else None)

    low = lax.rem(place.patch, 2) == 0
    for n in range(HALO):
        above, below = [], []
        for q in range(2):
            by_odd, by_even = odd_ref[n, q].astype(F32), even_ref[n, q].astype(F32)
            above.append(jnp.where(low, by_odd, by_even))
            below.append(jnp.where(low, by_even, by_odd))
        put_planes(x_ref, n, *above)
        put_planes(x_ref, HALO + n, *below)

    def x_of(r):
        return (x_ref, r + HALO) if r < 0 else (xin_ref, r) if r < rows else (x_ref, HALO + r - rows)

    def h1_of(r):
        if 2 <= r < rows - 2:
            return h1in_ref, r - 2
        if -1 <= r < 2:
            return h1_ref, r + 1
        return (h1_ref, 3 + r - (rows - 2)) if rows - 2 <= r <= rows else None

    def ci_of(i):
        if 1 <= i < half - 1:
            return ciin_ref, i - 1
        return (ci_ref, i + 2) if i < 1 else (ci_ref, 3 + i - (half - 1))

    def h2_of(r):
        if 4 <= r < rows - 4:
            return h2in_ref, r - 4
        return (h2_ref, r + 1) if r < 4 else (h2_ref, 5 + r - (rows - 4))

    def h3_of(r):
        return (h3in_ref, r - 6) if 6 <= r < rows - 6 else (h3_ref, r) if r < 6 else (h3_ref, 6 + r - (rows - 6))

    pairs = [-2, -1, 0, half - 1, half, half + 1]
    first_conv(x_of, h1_of, pool_ref, pairs.index, pairs, w_ref.at[0], ring, c1)
    coarse_in(pool_ref, down_ref, ci_of, pairs, mask_to(half), ring, c2)
    order = [-1, 0, 1, half - 2, half - 1, half]
    coarse_conv(ci_of, co_ref, order, coarse_ref, ring)
    wanted = [r for r in range(-1, rows + 1) if not 4 <= r < rows - 4]
    lift(co_ref, up_ref, order, h1_of, h2_of, mask_to(rows), wanted, ring)
    second_conv(h2_of, h3_of, [i for i in range(half) if not 3 <= i < half - 3], w_ref.at[1], own, c1)

    spread = jnp.transpose(jnp.broadcast_to(outp_ref[...].astype(F32), (128, c1)))
    lane = lax.broadcasted_iota(jnp.int32, (c1, 128), 1)
    pick = jnp.concatenate([jnp.where(lane == r, spread, 0.0).astype(BF16) for r in range(rows)], axis=0)
    parts = []
    for q in range(2):
        found = [h3_of(r) for r in range(rows)]
        parts.append(jnp.concatenate([ref[q, at] for ref, at in found], axis=1))
    sums = jnp.dot(jnp.concatenate(parts, axis=0), pick, preferred_element_type=F32)
    for q in range(2):
        flat_ref[pl.ds(q, own, stride=2), :] = sums[q * own : (q + 1) * own]
    network = jnp.transpose(flat_ref[...])[:rows]

    level = now_ref[...]
    after = next_ref[...]
    scale_in = 1.0 / jnp.sqrt(level * level + 1.0)
    scale_skip = 1.0 / (level * level + 1.0)
    scale_out = level * scale_in
    ratio = after / level
    spread_by = jnp.sqrt(level * level - after * after)
    here = pl.ds(pl.multiple_of(place.piece * 2 * own, 128), 2 * own)
    noisy = noisy_ref[:, here]
    denoised = scale_skip * noisy + scale_out * network
    out_ref[...] = denoised + ratio * (noisy - denoised) + spread_by * noise_ref[:, here]


def near(*arrays):
    return [pltpu.with_memory_space_constraint(a, pltpu.VMEM) for a in arrays]


def per_device(
    sizes,
    noisy_field, noise_draw, cond_features, sigma_now, sigma_next, field_proj,
    fine_kernels, coarse_kernel, down_proj, up_proj, out_proj,
):
    rows, cols, c1 = cond_features.shape
    c2 = down_proj.shape[1]
    patches, copies = sizes["patch"], sizes["fsdp"]
    pieces = 2 if copies % 2 == 0 and cols % 256 == 0 else 1
    if sizes["sub"] != 2 or rows < 16 or rows > 42 or rows % 2:
        raise ValueError("unsupported split")
    window = cols // pieces
    own = window // 2
    ring = own + PER
    half = rows // 2
    vmem = pl.BlockSpec(memory_space=pltpu.VMEM)
    where = dict(sizes=sizes, pieces=pieces)
    limit = lambda mib: pltpu.CompilerParams(vmem_limit_bytes=mib << 20)

    mine, tile, send = pl.pallas_call(
        functools.partial(embed_kernel, **where),
        out_shape=[
            pltpu.VMEM((rows, 2, own, c1), BF16),
            pltpu.VMEM((rows, 2, PER, c1), BF16),
            pltpu.VMEM((rows, 2, PER, c1), BF16),
        ],
        in_specs=[vmem] + [pl.BlockSpec(memory_space=pltpu.HBM)] * 3,
        out_specs=[vmem] * 3,
        scratch_shapes=[
            pltpu.VMEM((rows, window, c1), BF16),
            pltpu.VMEM((rows, EDGE, c1), BF16),
            pltpu.VMEM((rows, EDGE, c1), BF16),
            pltpu.VMEM((rows, cols), F32),
            pltpu.VMEM((1, c1), F32),
            pltpu.VMEM((cols, 128), BF16),
            pltpu.VMEM((rows, window, c1), F32),
            pltpu.VMEM((rows, 2 * EDGE, c1), F32),
            pltpu.SemaphoreType.DMA((5,)),
        ],
        compiler_params=limit(8),
        name="embed",
    )(sigma_now[None], *[pltpu.with_memory_space_constraint(a, pltpu.HBM) for a in (cond_features, noisy_field, field_proj[None])])

    got = lax.ppermute(send, "sub", [(0, 1), (1, 0)])

    packed = pl.pallas_call(
        pack_kernel,
        out_shape=pltpu.VMEM((2, 12 * c1, 2 * c1), BF16),
        in_specs=[vmem],
        out_specs=vmem,
        cost_estimate=pl.CostEstimate(flops=0, bytes_accessed=2 << 20, transcendentals=0),
        compiler_params=limit(4),
        name="pack",
    )(*near(fine_kernels))

    full, for_even, for_odd = pl.pallas_call(
        functools.partial(border_kernel, **where),
        out_shape=[
            pltpu.VMEM((rows, 2, PER, c1), BF16),
            pltpu.VMEM((HALO, 2, ring, c1), BF16),
            pltpu.VMEM((HALO, 2, ring, c1), BF16),
        ],
        in_specs=[vmem] * 3,
        out_specs=[vmem] * 3,
        compiler_params=limit(4),
        name="border",
    )(*near(mine, tile, got))

    def swap(rows_to_give, low):
        return lax.ppermute(rows_to_give, "patch", [pair for i in range(low, patches - 1, 2) for pair in ((i, i + 1), (i + 1, i))])

    odd = swap(for_odd, 1)
    even = swap(for_even, 0)

    weights = near(coarse_kernel.reshape(9 * c2, c2), down_proj, up_proj)
    work = 2 * ring * c1 * c1 * 18 * 2 * (half - 2) + 2 * ring * 9 * c2 * c2 * (half - 4)
    inner = pl.pallas_call(
        functools.partial(inner_kernel, **where),
        out_shape=[
            pltpu.VMEM((rows, 4, ring, c1), BF16),
            pltpu.VMEM((rows - 4, 2, ring, c1), BF16),
            pltpu.VMEM((half - 2, 3, ring, c2), BF16),
            pltpu.VMEM((rows - 8, 4, ring, c1), BF16),
            pltpu.VMEM((2, rows - 12, own, c1), BF16),
        ],
        in_specs=[vmem] * 6,
        out_specs=[vmem] * 5,
        scratch_shapes=[
            pltpu.VMEM(((half - 2) * ring, c1), BF16),
            pltpu.VMEM(((half - 4) * ring, c2), BF16),
        ],
        cost_estimate=pl.CostEstimate(flops=work * 2, bytes_accessed=4 << 20, transcendentals=0),
        compiler_params=limit(12),
        name="inner",
    )(*near(mine, full, packed), *weights)

    part = pl.pallas_call(
        functools.partial(outer_kernel, **where),
        out_shape=pltpu.VMEM((rows, window), F32),
        in_specs=[vmem] * 16,
        out_specs=vmem,
        scratch_shapes=[
            pltpu.VMEM((2 * HALO, 4, ring, c1), BF16),
            pltpu.VMEM((6 * ring, c1), BF16),
            pltpu.VMEM((6, 2, ring, c1), BF16),
            pltpu.VMEM((6, 3, ring, c2), BF16),
            pltpu.VMEM((6 * ring, c2), BF16),
            pltpu.VMEM((10, 4, ring, c1), BF16),
            pltpu.VMEM((2, 12, own, c1), BF16),
            pltpu.VMEM((window, 128), F32),
        ],
        compiler_params=pltpu.CompilerParams(vmem_limit_bytes=16 << 20),
        name="outer",
    )(sigma_now[None], sigma_next[None], *near(odd, even, *inner[:1], packed, *inner[1:]), *weights, *near(out_proj[None], noisy_field, noise_draw))
    if pieces == 1:
        return part
    other = lax.ppermute(part, "fsdp", [(i, i ^ 1) for i in range(copies)])
    first = lax.rem(lax.axis_index("fsdp"), pieces) == 0
    return jnp.where(first, jnp.concatenate([part, other], axis=1), jnp.concatenate([other, part], axis=1))


def solution(mesh):
    return jax.shard_map(
        functools.partial(per_device, dict(mesh.shape)),
        mesh=mesh,
        in_specs=(
            P(("groups", "patch"), "sub"),
            P(("groups", "patch"), "sub"),
            P(("groups", "patch"), "sub", None),
            P(),
            P(),
            P(),
            P(),
            P(),
            P(),
            P(),
            P(),
        ),
        out_specs=P(("groups", "patch"), "sub"),
        check_vma=False,
    )
```
